32 devices in a mesh: band: 4 (over y, core), space: 8 (over z, x).
Axes of the slice: x: 2, y: 2, z: 4, core: 2. Of those that a mesh axis runs over, the one named last changes fastest.
Arguments:
- states: float32 [256, 48, 1024], P('band', 'space'), may hold values from -6 to 6
- patch_ids: int32 [48, 32], P('space'), may hold values from 0 to 63
- metric_table: float32 [64, 96], replicated, may hold values from 0.5 to 2
- potential: float32 [48, 1024], P('space'), may hold values from -3 to 0
Outputs:
- orthonormal: float32 [256, 48, 1024], P(None, 'space', 'band')
The draws below stay inside these ranges and needn't reach their ends.
All inputs are finite; a program needn't handle non-finite values.
Results may differ from the reference program's by a relative error of at most 0.00014.
Values sent between devices are 32-bit elements; how exact they have to be, the bound alone decides.
A program may use at most 64 MiB of HBM per device.

```python
import math
import jax
import jax.numpy as jnp
from jax import lax

STATES = 256
DEGREE = 3
PATCHES = 64
NY = 32
NZ = 32
NX = 48
NYZ = 1024
NCELLS = 49152
N_BAND = 4


def draw_potential(key, part):
    planes = (jnp.arange(NX, dtype=jnp.float32) + 0.5) / NX
    noise = jax.random.uniform(key, (NX, NY * NZ), jnp.float32, -1.0, 0.0)
    ramp = -2.0 * planes
    return noise + ramp[:, None]


def set_ends(values, stream_key, smallest, top_value):
    index_at = [jax.random.randint(jax.random.fold_in(stream_key, axis), (), 0, length) for axis, length in enumerate(values.shape)]
    main_axis = values.shape.index(max(values.shape))
    neighbour = index_at[:main_axis] + [(index_at[main_axis] + 1) % values.shape[main_axis]] + index_at[main_axis + 1:]
    return values.at[tuple(index_at)].set(smallest).at[tuple(neighbour)].set(top_value)


def level_of(rng, extent, split, smallest, high):
    def one(dim, blocks):
        steps = jax.random.uniform(jax.random.fold_in(jax.random.fold_in(rng, 6), dim), (blocks,), jnp.float32, smallest / len(split), high / len(split))
        return jnp.repeat(jnp.exp(steps), extent[dim] // blocks).reshape((-1,) + (1,) * (len(extent) - dim - 1))

    level = one(*split[0])
    for cut in split[1:]:
        level = level * one(*cut)
    return level


def scatter_about(key, dims, scale, bound, split=(), held_as=jnp.bfloat16):
    values = scale * jax.random.normal(key, dims, jnp.float32)
    if split:
        values = values * level_of(key, dims, split, -0.22, 0.18)
    return jnp.clip(values, -bound, bound).astype(held_as)


def setup_inputs(seed: int = 0) -> dict:
    keys = jax.random.split(jax.random.key(seed), 5)
    states = scatter_about(keys[0], (STATES, NX, NYZ), 1.0, 6.0, ((0, 4), (1, 8)), jnp.float32)
    patch_ids = set_ends(jax.random.randint(keys[1], (NX, NY), 0, PATCHES), jax.random.fold_in(keys[1], 1), 0, PATCHES - 1).astype(jnp.int32)
    metric_table = jnp.clip(jnp.exp(jax.random.uniform(keys[2], (PATCHES, 3 * NZ), jnp.float32, math.log(0.5), math.log(2.0))), 0.5, 2.0)
    potential = draw_potential(jax.random.fold_in(keys[4], 71), 0)
    return {"states": states, "patch_ids": patch_ids, "metric_table": metric_table, "potential": potential}


CENTRE = 8.5
HALF_WIDTH = 7.5
OFFSETS = (-2, -1, 0, 1, 2)
WEIGHTS = (-1.0 / 12.0, 4.0 / 3.0, -2.5, 4.0 / 3.0, -1.0 / 12.0)

def second_difference(padded, axis, length):
    total = WEIGHTS[0] * lax.slice_in_dim(padded, 2 + OFFSETS[0], 2 + OFFSETS[0] + length, axis=axis)
    for offset, weight in zip(OFFSETS[1:], WEIGHTS[1:]):
        total = total + weight * lax.slice_in_dim(padded, 2 + offset, 2 + offset + length, axis=axis)
    return total

def hamiltonian(block, pot_grid, metric):
    x_pad = jnp.pad(block, ((0, 0), (2, 2), (0, 0), (0, 0)))
    y_pad = jnp.pad(block, ((0, 0), (0, 0), (2, 2), (0, 0)))
    z_pad = jnp.pad(block, ((0, 0), (0, 0), (0, 0), (2, 2)))
    x_term = second_difference(x_pad, 1, block.shape[1])
    y_term = second_difference(y_pad, 2, block.shape[2])
    z_term = second_difference(z_pad, 3, block.shape[3])
    kinetic = metric[0] * x_term + metric[1] * y_term + metric[2] * z_term
    return pot_grid * block - 0.5 * kinetic

def chebyshev(block, pot_grid, metric):
    applied = hamiltonian(block, pot_grid, metric)
    earlier = block
    current = (applied - CENTRE * block) / HALF_WIDTH
    for degree_step in range(DEGREE - 1):
        applied = hamiltonian(current, pot_grid, metric)
        following = 2.0 * (applied - CENTRE * current) / HALF_WIDTH - earlier
        earlier = current
        current = following
    return current

def reference(states, patch_ids, metric_table, potential):
    looked = metric_table[patch_ids]
    metric = looked.reshape(NX, NY, 3, NZ).transpose(2, 0, 1, 3)
    pot_grid = potential.reshape(NX, NY, NZ)
    group = STATES // N_BAND
    blocks = states.reshape(STATES // group, group, NX, NY, NZ)
    filtered = lax.map(lambda block: chebyshev(block, pot_grid, metric), blocks)
    flat = filtered.reshape(STATES, NX * NY * NZ)
    gram = jnp.dot(flat.astype(jnp.float32), flat.T.astype(jnp.float32), precision=lax.Precision.HIGHEST, preferred_element_type=jnp.float32) / NCELLS
    factor = jnp.linalg.cholesky(gram)
    result = lax.linalg.triangular_solve(factor, flat, left_side=True, lower=True)
    return result.reshape(STATES, NX, NY * NZ)
```

```python
import functools

import jax
import jax.numpy as jnp
from jax import lax
from jax.experimental import pallas as pl
from jax.experimental.pallas import tpu as pltpu
from jax.sharding import PartitionSpec as P

DEGREE = 3
NZ = 32


CENTRE = 8.5
HALF_WIDTH = 7.5
WEIGHTS = (-1.0 / 12.0, 4.0 / 3.0, -2.5, 4.0 / 3.0, -1.0 / 12.0)


MESH = pl.DeviceIdType.MESH
HIGHEST = lax.Precision.HIGHEST
BLOCK = 64
TILE = 8


def matmul(left, right, dims):
    return lax.dot_general(
        left, right, (dims, ((), ())), precision=HIGHEST, preferred_element_type=jnp.float32
    )


def factor_block(diagonal):
    size = diagonal.shape[0]
    rows = lax.broadcasted_iota(jnp.int32, (size, size), 0)
    columns = lax.broadcasted_iota(jnp.int32, (size, size), 1)
    unit = jnp.where(rows == columns, 1.0, 0.0).astype(jnp.float32)
    work = jnp.concatenate([diagonal, unit], axis=1)
    width = work.shape[1]
    in_tile = lax.broadcasted_iota(jnp.int32, (TILE, width), 0)
    done = []
    for start in range(0, size, TILE):
        count = size - start
        row_in = lax.broadcasted_iota(jnp.int32, (count, width), 0)
        panel = [
            jnp.broadcast_to(work[:, start + k : start + k + 1], (count, width))
            for k in range(TILE)
        ]
        scale = jnp.zeros((TILE, width), jnp.float32)
        for k in range(TILE):
            pivot = panel[k][k : k + 1, :]
            inverse = 1.0 / pivot
            scale = jnp.where(in_tile == k, 1.0 / jnp.sqrt(pivot), scale)
            weight = jnp.where(row_in > k, panel[k] * inverse, 0.0)
            for later in range(k + 1, TILE):
                panel[later] = panel[later] - weight * panel[later][k : k + 1, :]
            work = work - weight * work[k : k + 1, :]
        done.append(work[:TILE] * scale)
        work = work[TILE:]
    return jnp.concatenate(done, axis=0)[:, size:]


def inverse_factor(work_ref, size):
    rows = lax.broadcasted_iota(jnp.int32, (size, size), 0)
    columns = lax.broadcasted_iota(jnp.int32, (size, size), 1)
    work_ref[:, size:] = jnp.where(rows == columns, 1.0, 0.0).astype(jnp.float32)
    for first in range(0, size, BLOCK):
        last = first + BLOCK
        low = first // 128 * 128
        high = size + -(-last // 128) * 128
        small = factor_block(work_ref[first:last, first:last])
        solved = matmul(small, work_ref[first:last, low:high], ((1,), (0,)))
        work_ref[first:last, low:high] = solved
        if last < size:
            aligned = last // 128 * 128
            update = matmul(solved[:, aligned - low : size - low], solved, ((0,), (0,)))
            work_ref[last:, low:high] -= update[last - aligned :]


def reduce_gram(bands, spaces, cell_total, packed, near, far, mine, final, whole, send_sems, recv_sems):
    near_count, far_count = 2 * bands, spaces // 2
    share = packed.shape[0] // near_count
    band, space = lax.axis_index("band"), lax.axis_index("space")
    line = space // 2
    side = space - 2 * line
    place = 2 * band + side
    own = pl.ds(pl.multiple_of(place * share, share), share)

    def near_peer(offset):
        index = lax.rem(place + offset, near_count)
        return index, {"band": index // 2, "space": 2 * line + lax.rem(index, 2)}

    def far_peer(offset):
        return {"band": band, "space": 2 * lax.rem(line + offset, far_count) + side}

    def send(source, landing, stage, target):
        pltpu.make_async_remote_copy(
            src_ref=source,
            dst_ref=landing,
            send_sem=send_sems.at[stage],
            recv_sem=recv_sems.at[stage],
            device_id=target,
            device_id_type=MESH,
        ).start()

    for offset in range(1, near_count):
        index, target = near_peer(offset)
        rows = pl.ds(pl.multiple_of(index * share, share), share)
        send(packed.at[rows], near.at[offset - 1], 0, target)
    pltpu.make_async_copy(near, near, recv_sems.at[0]).wait()
    mine[...] = jnp.sum(near[...], axis=0) + packed[own]
    for offset in range(1, far_count):
        send(mine, far.at[line], 1, far_peer(offset))
    others = far.at[0 : far_count - 1]
    pltpu.make_async_copy(others, others, recv_sems.at[1]).wait()
    far[line] = mine[...]
    final[...] = jnp.sum(far[...], axis=0) / cell_total
    for offset in range(1, near_count):
        send(final, whole.at[own], 2, near_peer(offset)[1])
    rest = whole.at[0 : whole.shape[0] - share]
    pltpu.make_async_copy(rest, rest, recv_sems.at[2]).wait()
    whole[own] = final[...]

    def settle():
        pltpu.make_async_copy(near, near, send_sems.at[0]).wait()
        pltpu.make_async_copy(others, others, send_sems.at[1]).wait()
        pltpu.make_async_copy(near, near, send_sems.at[2]).wait()

    return settle


FIRST = 4.0 / 3.0
RATIO = 1.0 / 16.0
REACH = 2
LANES = 128
GROUP = 4


def split(value):
    high = value.astype(jnp.bfloat16)
    return high, (value - high.astype(jnp.float32)).astype(jnp.bfloat16)


def product(left, right, dims):
    left_high, left_low = left
    right_high, right_low = right

    def one(first, second):
        return lax.dot_general(first, second, (dims, ((), ())), preferred_element_type=jnp.float32)

    return one(left_high, right_high) + (one(left_high, right_low) + one(left_low, right_high))


def filter_kernel(
    bands, spaces, cell_total, states, ids, table_in, potential, high_out, low_out, inverse_high,
    inverse_low, out, high, low, packed, near, far, mine, final, whole, work, grids, last, cells, near_ids, near_pot,
    table, tables, first_sems, base_send, base_recv, in_send, in_recv, keep_sems, halo_send, halo_recv, out_send,
    out_recv, store_sems, gram_send, gram_recv,
):
    planes, held, plane_cells = states.shape
    half = held // 2
    chunks = half // TILE
    span = 4 * planes
    share = plane_cells // bands
    tiles = plane_cells // LANES
    band = lax.axis_index("band")
    space = lax.axis_index("space")
    side = lax.rem(space, 2)
    partner = space + 1 - 2 * side
    outward = space + 4 * side - 2
    across = space - 4 * side + 2
    has_outward = jnp.logical_and(outward >= 0, outward < spaces)
    has_across = jnp.logical_and(across >= 0, across < spaces)

    def to(target_band, target_space):
        return {"band": target_band, "space": target_space}

    own, theirs = 1 + side, 2 - side
    firsts = [
        pltpu.make_async_copy(source, landing, first_sems.at[number])
        for number, (source, landing) in enumerate(
            ((ids, near_ids.at[own]), (potential, near_pot.at[own]), (table_in, table))
        )
    ]
    for copy in firsts:
        copy.start()

    barrier = pltpu.get_barrier_semaphore()
    for turn in range(bands):
        target = lax.rem(band + turn, bands)
        if turn:
            pl.semaphore_signal(
                barrier, inc=1, device_id=to(target, space), device_id_type=MESH
            )
        pl.semaphore_signal(barrier, inc=1, device_id=to(target, partner), device_id_type=MESH)
    lines = spaces // 2
    for offset in range(1, lines):
        pl.semaphore_signal(
            barrier,
            inc=1,
            device_id=to(band, 2 * lax.rem(space // 2 + offset, lines) + side),
            device_id_type=MESH,
        )
    pl.semaphore_wait(barrier, 2 * bands + lines - 2)

    def slab(place):
        return pl.ds(place * planes, planes)

    def rows_of(part, chunk):
        return pl.ds(pl.multiple_of(part * half + chunk * TILE, TILE), TILE)

    def remote(source, landing, send_sem, recv_sem, target):
        return pltpu.make_async_remote_copy(
            src_ref=source,
            dst_ref=landing,
            send_sem=send_sem,
            recv_sem=recv_sem,
            device_id=to(band, target),
            device_id_type=MESH,
        )

    own_landing, passed_landing = 3 * (1 - side), 3 * side
    base_sends = []
    for kind, (source, landing) in enumerate(((ids, near_ids), (potential, near_pot))):
        base_sends.append(
            (
                remote(source, landing.at[own], base_send.at[kind, 0], base_recv.at[kind, 0], partner),
                remote(source, landing.at[own_landing], base_send.at[kind, 1], base_recv.at[kind, 1], outward),
                remote(
                    landing.at[theirs], landing.at[passed_landing],
                    base_send.at[kind, 2], base_recv.at[kind, 2], across,
                ),
            )
        )
    enter, keep, halo_own, halo_passed = [], [], [], []
    for chunk in range(chunks):
        grid = grids.at[0, chunk]
        kept = states.at[:, rows_of(side, chunk)]
        enter.append(
            remote(
                states.at[:, rows_of(1 - side, chunk)], grid.at[slab(own)],
                in_send.at[chunk], in_recv.at[chunk], partner,
            )
        )
        keep.append(pltpu.make_async_copy(kept, grid.at[slab(own)], keep_sems.at[chunk]))
        halo_own.append(
            remote(
                kept, grid.at[slab(own_landing)],
                halo_send.at[0, chunk], halo_recv.at[0, chunk], outward,
            )
        )
        halo_passed.append(
            remote(
                grid.at[slab(theirs)], grid.at[slab(passed_landing)],
                halo_send.at[1, chunk], halo_recv.at[1, chunk], across,
            )
        )

    def begin(chunk):
        enter[chunk].start()

        @pl.when(has_outward)
        def _():
            halo_own[chunk].start()

    for kind in range(2):
        base_sends[kind][0].start()

    @pl.when(has_outward)
    def _():
        for kind in range(2):
            base_sends[kind][1].start()

    for chunk in range(min(2, chunks)):
        begin(chunk)
    for chunk in range(chunks):
        keep[chunk].start()
    for copy in firsts:
        copy.wait()
    missing_places = ((0, space < 2), (3, space >= spaces - 2))
    for place, missing in missing_places:

        @pl.when(missing)
        def _():
            near_ids[place] = jnp.zeros(near_ids.shape[1:], jnp.int32)
            near_pot[place] = jnp.zeros(near_pot.shape[1:], jnp.float32)
            for chunk in range(chunks):
                for plane in range(place * planes, (place + 1) * planes):
                    grids[0, chunk, plane] = jnp.zeros((TILE, plane_cells), jnp.float32)

    patches = table.shape[0]
    depth = table.shape[1] // 3
    source = lax.broadcasted_iota(jnp.int32, (table.shape[1], 3 * LANES), 0)
    lane_of = lax.broadcasted_iota(jnp.int32, (table.shape[1], 3 * LANES), 1)
    wanted = lane_of // LANES * depth + lane_of % depth
    spread = jnp.where(source == wanted, 1.0, 0.0).astype(jnp.float32)
    tables[...] = matmul(table[...], spread, ((1,), (0,)))

    for kind in range(2):
        base_sends[kind][0].wait_recv()

    @pl.when(has_across)
    def _():
        for kind in range(2):
            base_sends[kind][2].start()
        for kind in range(2):
            base_sends[kind][1].wait_recv()

    @pl.when(has_outward)
    def _():
        for kind in range(2):
            base_sends[kind][2].wait_recv()

    row_source = lax.broadcasted_iota(jnp.int32, (ids.shape[1], plane_cells), 0)
    row_lane = lax.broadcasted_iota(jnp.int32, (ids.shape[1], plane_cells), 1)
    row_spread = jnp.where(row_source == row_lane // NZ, 1.0, 0.0).astype(jnp.float32)

    def make_cells(place, carry):
        patch = matmul(near_ids[place].astype(jnp.float32), row_spread, ((1,), (0,)))
        zero = jnp.zeros(patch.shape, jnp.float32)

        def look(step, metric):
            rows = tables[pl.ds(pl.multiple_of(TILE * step, TILE), TILE), :]
            for row in range(TILE):
                here = patch == (TILE * step + row).astype(jnp.float32)
                metric = tuple(
                    jnp.where(
                        here,
                        jnp.concatenate(
                            [rows[row : row + 1, kind * LANES : (kind + 1) * LANES]] * tiles, axis=1
                        ),
                        value,
                    )
                    for kind, value in enumerate(metric)
                )
            return metric

        metric = lax.fori_loop(0, patches // TILE, look, (zero, zero, zero))
        kinetic = [value * (-1.0 / HALF_WIDTH) for value in metric]
        centre = (near_pot[place] - CENTRE) * (2.0 / HALF_WIDTH) + WEIGHTS[2] * (
            kinetic[0] + kinetic[1] + kinetic[2]
        )
        for kind, value in enumerate([centre] + [FIRST * value for value in kinetic]):
            for plane in range(planes):
                cells[place * planes + plane, kind : kind + 1] = value[plane : plane + 1]
        return carry

    lax.fori_loop(0, 4, make_cells, 0)
    for place, missing in missing_places:

        @pl.when(missing)
        def _():
            for plane in range(place * planes, (place + 1) * planes):
                cells[plane] = jnp.zeros(cells.shape[1:], jnp.float32)

    lane = lax.broadcasted_iota(jnp.int32, (TILE, LANES), 1)
    depth_at = lane % NZ
    zero_tile = jnp.zeros((TILE, LANES), jnp.float32)

    def mask(inside, weight):
        return jnp.where(inside, weight, 0.0).astype(jnp.float32)

    back_one, fore_one = mask(depth_at >= 1, 1.0), mask(depth_at < NZ - 1, 1.0)
    back_two, fore_two = mask(depth_at >= 2, RATIO), mask(depth_at < NZ - 2, RATIO)
    first_row, front_half, not_last = lane < NZ, lane < 2 * NZ, lane < 3 * NZ

    def roll(value, amount):
        return pltpu.roll(value, amount, axis=1)

    def apply(step, chunk):
        edge = REACH * (step + 1)

        def some_planes(number, carry):
            first = edge + GROUP * number
            results = []
            state = []
            for k in range(GROUP):
                value = grids[step, chunk, first + k, :, 0:LANES]
                state.append((value, zero_tile, roll(value, 2 * NZ), roll(value, 3 * NZ), zero_tile))
            for tile in range(tiles):
                columns = slice(tile * LANES, (tile + 1) * LANES)
                for k in range(GROUP):
                    here = first + k
                    value, two_before, two_here, one_after, one_before = state[k]
                    one_here = roll(value, NZ)
                    if tile < tiles - 1:
                        following = grids[step, chunk, here, :, (tile + 1) * LANES : (tile + 2) * LANES]
                        two_after, one_next = roll(following, 2 * NZ), roll(following, 3 * NZ)
                    else:
                        following, two_after, one_next = None, zero_tile, zero_tile
                    state[k] = (following, two_here, two_after, one_next, one_here)

                    def plane(shift):
                        return grids[step, chunk, here + shift, :, columns]

                    def cell(kind):
                        return cells[here, kind : kind + 1, columns]

                    total = cell(0) * value
                    total = total + cell(1) * (
                        (plane(-1) + plane(1)) - (plane(-2) + plane(2)) * RATIO
                    )
                    near = jnp.where(first_row, one_before, one_here) + jnp.where(
                        not_last, one_after, one_next
                    )
                    far = two_here + jnp.where(front_half, two_before, two_after)
                    total = total + cell(2) * (near - far * RATIO)
                    along = (back_one * roll(value, 1) + fore_one * roll(value, LANES - 1)) - (
                        back_two * roll(value, 2) + fore_two * roll(value, LANES - 2)
                    )
                    total = total + cell(3) * along
                    if step > 0:
                        total = total - grids[step - 1, chunk, here, :, columns]
                    else:
                        total = total * 0.5
                    results.append((here, columns, total))
            for here, columns, total in results:
                if step < DEGREE - 1:
                    grids[step + 1, chunk, here, :, columns] = total
                else:
                    last[chunk, here - planes, :, columns] = total
            return carry

        lax.fori_loop(0, (span - 2 * edge) // GROUP, some_planes, 0)

    def leave(chunk):
        rows = pl.ds(pl.multiple_of(band * held + side * half + chunk * TILE, TILE), TILE)
        for turn in range(bands):
            target = lax.rem(band + turn, bands)
            columns = pl.ds(pl.multiple_of(target * share, share), share)
            for other in (1, 0):
                source = last.at[chunk, slab(side if other == 0 else 1 - side), :, columns]
                landing = out.at[:, rows, :]
                if turn == 0 and other == 0:
                    pltpu.make_async_copy(source, landing, out_recv.at[0]).start()
                else:
                    pltpu.make_async_remote_copy(
                        src_ref=source,
                        dst_ref=landing,
                        send_sem=out_send.at[0],
                        recv_sem=out_recv.at[0],
                        device_id=to(target, space if other == 0 else partner),
                        device_id_type=MESH,
                    ).start()

    def finish(chunk):
        @pl.when(has_across)
        def _():
            halo_own[chunk].wait_recv()

        @pl.when(has_outward)
        def _():
            halo_passed[chunk].wait_recv()

        for step in range(DEGREE):
            apply(step, chunk)
        leave(chunk)

    for chunk in range(chunks):
        keep[chunk].wait()
        enter[chunk].wait_recv()

        @pl.when(has_across)
        def _():
            halo_passed[chunk].start()

        if chunk + 2 < chunks:
            begin(chunk + 2)
        if chunk > 0:
            finish(chunk - 1)
    finish(chunks - 1)

    for kind in range(2):
        base_sends[kind][0].wait_send()
    for chunk in range(chunks):
        enter[chunk].wait_send()

    @pl.when(has_outward)
    def _():
        for kind in range(2):
            base_sends[kind][1].wait_send()
        for chunk in range(chunks):
            halo_own[chunk].wait_send()

    @pl.when(has_across)
    def _():
        for kind in range(2):
            base_sends[kind][2].wait_send()
        for chunk in range(chunks):
            halo_passed[chunk].wait_send()

    pltpu.make_async_copy(out, out, out_recv.at[0]).wait()
    size = out.shape[1]
    middle = size // 2
    upper, lower = None, None
    for plane in range(planes):
        plane_high, plane_low = split(out[plane])
        high[plane], low[plane] = plane_high, plane_low
        both = (plane_high, plane_low)
        top = (plane_high[:middle], plane_low[:middle])
        bottom = (plane_high[middle:], plane_low[middle:])
        term = product(top, both, ((1,), (1,)))
        upper = term if upper is None else upper + term
        term = product(bottom, bottom, ((1,), (1,)))
        lower = term if lower is None else lower + term
    packed[:, :size] = upper
    packed[:, size:] = lower
    stores = [
        pltpu.make_async_copy(high, high_out, store_sems.at[0]),
        pltpu.make_async_copy(low, low_out, store_sems.at[1]),
    ]
    for copy in stores:
        copy.start()
    settle = reduce_gram(
        bands, spaces, cell_total, packed, near, far, mine, final, whole, gram_send, gram_recv
    )
    work[:middle, :size] = whole[:, :size]
    work[middle:, middle:size] = whole[:, size:]
    inverse_factor(work, size)
    inverse_high[...], inverse_low[...] = split(work[:, size:])
    settle()
    for copy in stores:
        copy.wait()
    sent = out.at[:, 0 : out.shape[1] - out.shape[1] // (2 * bands), :]
    pltpu.make_async_copy(sent, sent, out_send.at[0]).wait()


def filtered_and_inverse(states, ids, table, potential):
    planes, held, plane_cells = states.shape
    bands = lax.axis_size("band")
    spaces = lax.axis_size("space")
    chunks = held // 2 // TILE
    total = held * bands
    share = total // 2 // (2 * bands)
    if planes != REACH * DEGREE:
        raise ValueError("slab depth")
    dma = pltpu.SemaphoreType.DMA
    vmem = pl.BlockSpec(memory_space=pltpu.VMEM)
    hbm = pl.BlockSpec(memory_space=pltpu.HBM)
    regrouped = (planes, total, plane_cells // bands)
    packed = (total // 2, total // 2 * 3)
    return pl.pallas_call(
        functools.partial(filter_kernel, bands, spaces, float(planes * plane_cells * spaces)),
        out_shape=tuple(
            jax.ShapeDtypeStruct(shape, jnp.bfloat16)
            for shape in (regrouped, regrouped, (total, total), (total, total))
        ),
        in_specs=[hbm] * 4,
        out_specs=(hbm, hbm, vmem, vmem),
        scratch_shapes=[
            pltpu.VMEM(regrouped, jnp.float32),
            pltpu.VMEM(regrouped, jnp.bfloat16),
            pltpu.VMEM(regrouped, jnp.bfloat16),
            pltpu.VMEM(packed, jnp.float32),
            pltpu.VMEM((2 * bands - 1, share, packed[1]), jnp.float32),
            pltpu.VMEM((spaces // 2, share, packed[1]), jnp.float32),
            pltpu.VMEM((share, packed[1]), jnp.float32),
            pltpu.VMEM((share, packed[1]), jnp.float32),
            pltpu.VMEM(packed, jnp.float32),
            pltpu.VMEM((total, 2 * total), jnp.float32),
            pltpu.VMEM((DEGREE, chunks, 4 * planes, TILE, plane_cells), jnp.float32),
            pltpu.VMEM((chunks, 2 * planes, TILE, plane_cells), jnp.float32),
            pltpu.VMEM((4 * planes, 4, plane_cells), jnp.float32),
            pltpu.VMEM((4,) + ids.shape, jnp.int32),
            pltpu.VMEM((4,) + potential.shape, jnp.float32),
            pltpu.VMEM(table.shape, jnp.float32),
            pltpu.VMEM((table.shape[0], 3 * LANES), jnp.float32),
            dma((3,)),
            dma((2, 3)),
            dma((2, 3)),
            dma((chunks,)),
            dma((chunks,)),
            dma((chunks,)),
            dma((2, chunks)),
            dma((2, chunks)),
            dma((1,)),
            dma((1,)),
            dma((2,)),
            dma((3,)),
            dma((3,)),
        ],
        compiler_params=pltpu.CompilerParams(
            collective_id=0, has_side_effects=True, vmem_limit_bytes=60 * 2**20
        ),
        name="filter_factor",
    )(states, ids, table, potential)


def solve_kernel(inverse_high, inverse_low, high, low, result):
    result[0] = product(
        (inverse_high[...], inverse_low[...]), (high[0], low[0]), ((1,), (0,))
    )


def solved(high, low, inverse_high, inverse_low):
    planes, size, width = high.shape
    whole = pl.BlockSpec((size, size), lambda plane: (0, 0))
    block = pl.BlockSpec((1, size, width), lambda plane: (plane, 0, 0))
    return pl.pallas_call(
        solve_kernel,
        grid=(planes,),
        out_shape=jax.ShapeDtypeStruct(high.shape, jnp.float32),
        in_specs=[whole, whole, block, block],
        out_specs=block,
        name="solve",
    )(inverse_high, inverse_low, high, low)


def on_device(states, patch_ids, metric_table, potential):
    parts = filtered_and_inverse(states.transpose(1, 0, 2), patch_ids, metric_table, potential)
    return solved(*parts).transpose(1, 0, 2)


def solution(mesh):
    return jax.shard_map(
        on_device,
        mesh=mesh,
        in_specs=(P("band", "space", None), P("space", None), P(), P("space", None)),
        out_specs=P(None, "space", "band"),
        check_vma=False,
    )
```

```python
import functools

import jax
import jax.numpy as jnp
from jax import lax
from jax.experimental import pallas as pl
from jax.experimental.pallas import tpu as pltpu
from jax.sharding import PartitionSpec as P

DEGREE = 3
NZ = 32


CENTRE = 8.5
HALF_WIDTH = 7.5
WEIGHTS = (-1.0 / 12.0, 4.0 / 3.0, -2.5, 4.0 / 3.0, -1.0 / 12.0)


MESH = pl.DeviceIdType.MESH
HIGHEST = lax.Precision.HIGHEST
BLOCK = 64
TILE = 8
LANES = 128


def matmul(left, right, dims):
    return lax.dot_general(
        left, right, (dims, ((), ())), precision=HIGHEST, preferred_element_type=jnp.float32
    )


def factor_block(diagonal):
    size = diagonal.shape[0]
    rows = lax.broadcasted_iota(jnp.int32, (size, size), 0)
    columns = lax.broadcasted_iota(jnp.int32, (size, size), 1)
    unit = jnp.where(rows == columns, 1.0, 0.0).astype(jnp.float32)
    work = jnp.concatenate([diagonal, unit], axis=1)
    width = work.shape[1]
    in_tile = lax.broadcasted_iota(jnp.int32, (TILE, width), 0)
    done = []
    for start in range(0, size, TILE):
        count = size - start
        row_in = lax.broadcasted_iota(jnp.int32, (count, width), 0)
        panel = [
            jnp.broadcast_to(work[:, start + k : start + k + 1], (count, width))
            for k in range(TILE)
        ]
        scale = jnp.zeros((TILE, width), jnp.float32)
        for k in range(TILE):
            pivot = panel[k][k : k + 1, :]
            inverse = 1.0 / pivot
            scale = jnp.where(in_tile == k, 1.0 / jnp.sqrt(pivot), scale)
            weight = jnp.where(row_in > k, panel[k] * inverse, 0.0)
            for later in range(k + 1, TILE):
                panel[later] = panel[later] - weight * panel[later][k : k + 1, :]
            work = work - weight * work[k : k + 1, :]
        done.append(work[:TILE] * scale)
        work = work[TILE:]
    return jnp.concatenate(done, axis=0)[:, size:]


def start_factor(pending, size):
    rows = lax.broadcasted_iota(jnp.int32, (size, 2 * size), 0)
    columns = lax.broadcasted_iota(jnp.int32, (size, 2 * size), 1)
    pending[...] = jnp.where(columns == rows + size, 1.0, 0.0).astype(jnp.float32)


def factor_rows(gram, pending, inverse, first, size):
    last = first + BLOCK
    low = first // LANES * LANES
    high = size + -(-last // LANES) * LANES
    current = jnp.concatenate(
        [
            gram[first:last, low:size] + pending[first:last, low:size],
            pending[first:last, size:high],
        ],
        axis=1,
    )
    small = factor_block(current[:, first - low : last - low])
    rows = matmul(small, current, ((1,), (0,)))
    inverse[first:last, 0 : high - size] = rows[:, size - low :]
    if last < size:
        aligned = last // LANES * LANES
        update = matmul(rows[:, aligned - low : size - low], rows, ((0,), (0,)))
        pending[last:, low:high] -= update[last - aligned :]


def start_reduction(bands, spaces, cell_total, local, near, far, mine, final, gram, send_sems, recv_sems):
    size = local.shape[0]
    near_count, far_count = 2 * bands, spaces // 2
    pieces = near.shape[0]
    depth = size // pieces
    share = depth // near_count
    band, space = lax.axis_index("band"), lax.axis_index("space")
    line = space // 2
    side = space - 2 * line
    place = 2 * band + side

    def rows_of(piece, index):
        return pl.ds(pl.multiple_of(piece * depth + index * share, share), share)

    def columns_of(piece):
        return slice(piece * depth // LANES * LANES, size)

    def near_peer(offset):
        index = lax.rem(place + offset, near_count)
        return index, {"band": index // 2, "space": 2 * line + lax.rem(index, 2)}

    def far_peer(offset):
        return {"band": band, "space": 2 * lax.rem(line + offset, far_count) + side}

    def send(source, landing, stage, piece, target):
        pltpu.make_async_remote_copy(
            src_ref=source,
            dst_ref=landing,
            send_sem=send_sems.at[stage, piece],
            recv_sem=recv_sems.at[stage, piece],
            device_id=target,
            device_id_type=MESH,
        ).start()

    def bytes_of(stage, piece):
        columns = columns_of(piece)
        if stage == 1:
            return far.at[piece, 0 : far_count - 1, :, columns]
        return near.at[piece, :, :, columns]

    def wait(sems, stage, piece):
        moved = bytes_of(stage, piece)
        pltpu.make_async_copy(moved, moved, sems.at[stage, piece]).wait()

    for piece in range(pieces):
        columns = columns_of(piece)
        for offset in range(1, near_count):
            index, target = near_peer(offset)
            send(
                local.at[rows_of(piece, index), columns], near.at[piece, offset - 1, :, columns],
                0, piece, target,
            )
    for piece in range(pieces):
        columns = columns_of(piece)
        wait(recv_sems, 0, piece)
        mine[piece, :, columns] = (
            jnp.sum(near[piece, :, :, columns], axis=0) + local[rows_of(piece, place), columns]
        )
        for offset in range(1, far_count):
            send(
                mine.at[piece, :, columns], far.at[piece, line, :, columns], 1, piece,
                far_peer(offset),
            )
    for piece in range(pieces):
        columns = columns_of(piece)
        wait(recv_sems, 1, piece)
        far[piece, line, :, columns] = mine[piece, :, columns]
        final[piece, :, columns] = jnp.sum(far[piece, :, :, columns], axis=0) / cell_total
        for offset in range(1, near_count):
            send(
                final.at[piece, :, columns], gram.at[rows_of(piece, place), columns], 2, piece,
                near_peer(offset)[1],
            )

    def arrived(piece):
        columns = columns_of(piece)
        wait(recv_sems, 2, piece)
        gram[rows_of(piece, place), columns] = final[piece, :, columns]

    def settle():
        for stage in range(3):
            for piece in range(pieces):
                wait(send_sems, stage, piece)

    return depth, arrived, settle


FIRST = 4.0 / 3.0
RATIO = 1.0 / 16.0
REACH = 2
GROUP = 4


def split(value):
    high = value.astype(jnp.bfloat16)
    return high, (value - high.astype(jnp.float32)).astype(jnp.bfloat16)


def product(left, right, dims):
    left_high, left_low = left
    right_high, right_low = right

    def one(first, second):
        return lax.dot_general(first, second, (dims, ((), ())), preferred_element_type=jnp.float32)

    return one(left_high, right_high) + (one(left_high, right_low) + one(left_low, right_high))


def filter_kernel(
    bands, spaces, cell_total, states, ids, table_in, potential, result, out, high, low, staged,
    local, near, far, mine, final, gram, pending, inverse, grids, last, cells, near_ids, near_pot,
    table, tables, first_sems, base_send, base_recv, in_send, in_recv, keep_sems, halo_send, halo_recv, out_send,
    out_recv, store_sems, gram_send, gram_recv,
):
    planes, held, plane_cells = states.shape
    half = held // 2
    chunks = half // TILE
    span = 4 * planes
    share = plane_cells // bands
    tiles = plane_cells // LANES
    band = lax.axis_index("band")
    space = lax.axis_index("space")
    side = lax.rem(space, 2)
    partner = space + 1 - 2 * side
    outward = space + 4 * side - 2
    across = space - 4 * side + 2
    has_outward = jnp.logical_and(outward >= 0, outward < spaces)
    has_across = jnp.logical_and(across >= 0, across < spaces)

    def to(target_band, target_space):
        return {"band": target_band, "space": target_space}

    own, theirs = 1 + side, 2 - side
    firsts = [
        pltpu.make_async_copy(source, landing, first_sems.at[number])
        for number, (source, landing) in enumerate(
            ((ids, near_ids.at[own]), (potential, near_pot.at[own]), (table_in, table))
        )
    ]
    for copy in firsts:
        copy.start()

    barrier = pltpu.get_barrier_semaphore()
    for turn in range(bands):
        target = lax.rem(band + turn, bands)
        if turn:
            pl.semaphore_signal(
                barrier, inc=1, device_id=to(target, space), device_id_type=MESH
            )
        pl.semaphore_signal(barrier, inc=1, device_id=to(target, partner), device_id_type=MESH)
    lines = spaces // 2
    for offset in range(1, lines):
        pl.semaphore_signal(
            barrier,
            inc=1,
            device_id=to(band, 2 * lax.rem(space // 2 + offset, lines) + side),
            device_id_type=MESH,
        )
    pl.semaphore_wait(barrier, 2 * bands + lines - 2)

    def slab(place):
        return pl.ds(place * planes, planes)

    def rows_of(part, chunk):
        return pl.ds(pl.multiple_of(part * half + chunk * TILE, TILE), TILE)

    def remote(source, landing, send_sem, recv_sem, target):
        return pltpu.make_async_remote_copy(
            src_ref=source,
            dst_ref=landing,
            send_sem=send_sem,
            recv_sem=recv_sem,
            device_id=to(band, target),
            device_id_type=MESH,
        )

    own_landing, passed_landing = 3 * (1 - side), 3 * side
    base_sends = []
    for kind, (source, landing) in enumerate(((ids, near_ids), (potential, near_pot))):
        base_sends.append(
            (
                remote(source, landing.at[own], base_send.at[kind, 0], base_recv.at[kind, 0], partner),
                remote(source, landing.at[own_landing], base_send.at[kind, 1], base_recv.at[kind, 1], outward),
                remote(
                    landing.at[theirs], landing.at[passed_landing],
                    base_send.at[kind, 2], base_recv.at[kind, 2], across,
                ),
            )
        )
    enter, keep, halo_own, halo_passed = [], [], [], []
    for chunk in range(chunks):
        grid = grids.at[0, chunk]
        kept = states.at[:, rows_of(side, chunk)]
        enter.append(
            remote(
                states.at[:, rows_of(1 - side, chunk)], grid.at[slab(own)],
                in_send.at[chunk], in_recv.at[chunk], partner,
            )
        )
        keep.append(pltpu.make_async_copy(kept, grid.at[slab(own)], keep_sems.at[chunk]))
        halo_own.append(
            remote(
                kept, grid.at[slab(own_landing)],
                halo_send.at[0, chunk], halo_recv.at[0, chunk], outward,
            )
        )
        halo_passed.append(
            remote(
                grid.at[slab(theirs)], grid.at[slab(passed_landing)],
                halo_send.at[1, chunk], halo_recv.at[1, chunk], across,
            )
        )

    def begin(chunk):
        enter[chunk].start()

        @pl.when(has_outward)
        def _():
            halo_own[chunk].start()

    for kind in range(2):
        base_sends[kind][0].start()

    @pl.when(has_outward)
    def _():
        for kind in range(2):
            base_sends[kind][1].start()

    for chunk in range(min(2, chunks)):
        begin(chunk)
    for chunk in range(chunks):
        keep[chunk].start()
    for copy in firsts:
        copy.wait()
    missing_places = ((0, space < 2), (3, space >= spaces - 2))
    for place, missing in missing_places:

        @pl.when(missing)
        def _():
            near_ids[place] = jnp.zeros(near_ids.shape[1:], jnp.int32)
            near_pot[place] = jnp.zeros(near_pot.shape[1:], jnp.float32)
            for chunk in range(chunks):
                for plane in range(place * planes, (place + 1) * planes):
                    grids[0, chunk, plane] = jnp.zeros((TILE, plane_cells), jnp.float32)

    patches = table.shape[0]
    depth = table.shape[1] // 3
    source = lax.broadcasted_iota(jnp.int32, (table.shape[1], 3 * LANES), 0)
    lane_of = lax.broadcasted_iota(jnp.int32, (table.shape[1], 3 * LANES), 1)
    wanted = lane_of // LANES * depth + lane_of % depth
    spread = jnp.where(source == wanted, 1.0, 0.0).astype(jnp.float32)
    tables[...] = matmul(table[...], spread, ((1,), (0,)))

    for kind in range(2):
        base_sends[kind][0].wait_recv()

    @pl.when(has_across)
    def _():
        for kind in range(2):
            base_sends[kind][2].start()
        for kind in range(2):
            base_sends[kind][1].wait_recv()

    @pl.when(has_outward)
    def _():
        for kind in range(2):
            base_sends[kind][2].wait_recv()

    row_source = lax.broadcasted_iota(jnp.int32, (ids.shape[1], plane_cells), 0)
    row_lane = lax.broadcasted_iota(jnp.int32, (ids.shape[1], plane_cells), 1)
    row_spread = jnp.where(row_source == row_lane // NZ, 1.0, 0.0).astype(jnp.float32)

    def make_cells(place, carry):
        patch = matmul(near_ids[place].astype(jnp.float32), row_spread, ((1,), (0,)))
        zero = jnp.zeros(patch.shape, jnp.float32)

        def look(step, metric):
            rows = tables[pl.ds(pl.multiple_of(TILE * step, TILE), TILE), :]
            for row in range(TILE):
                here = patch == (TILE * step + row).astype(jnp.float32)
                metric = tuple(
                    jnp.where(
                        here,
                        jnp.concatenate(
                            [rows[row : row + 1, kind * LANES : (kind + 1) * LANES]] * tiles, axis=1
                        ),
                        value,
                    )
                    for kind, value in enumerate(metric)
                )
            return metric

        metric = lax.fori_loop(0, patches // TILE, look, (zero, zero, zero))
        kinetic = [value * (-1.0 / HALF_WIDTH) for value in metric]
        centre = (near_pot[place] - CENTRE) * (2.0 / HALF_WIDTH) + WEIGHTS[2] * (
            kinetic[0] + kinetic[1] + kinetic[2]
        )
        for kind, value in enumerate([centre] + [FIRST * value for value in kinetic]):
            for plane in range(planes):
                cells[place * planes + plane, kind : kind + 1] = value[plane : plane + 1]
        return carry

    lax.fori_loop(0, 4, make_cells, 0)
    for place, missing in missing_places:

        @pl.when(missing)
        def _():
            for plane in range(place * planes, (place + 1) * planes):
                cells[plane] = jnp.zeros(cells.shape[1:], jnp.float32)

    start_factor(pending, pending.shape[0])
    lane = lax.broadcasted_iota(jnp.int32, (TILE, LANES), 1)
    depth_at = lane % NZ
    zero_tile = jnp.zeros((TILE, LANES), jnp.float32)

    def mask(inside, weight):
        return jnp.where(inside, weight, 0.0).astype(jnp.float32)

    back_one, fore_one = mask(depth_at >= 1, 1.0), mask(depth_at < NZ - 1, 1.0)
    back_two, fore_two = mask(depth_at >= 2, RATIO), mask(depth_at < NZ - 2, RATIO)
    first_row, front_half, not_last = lane < NZ, lane < 2 * NZ, lane < 3 * NZ

    def roll(value, amount):
        return pltpu.roll(value, amount, axis=1)

    def apply(step, chunk):
        edge = REACH * (step + 1)

        def some_planes(number, carry):
            first = edge + GROUP * number
            results = []
            state = []
            for k in range(GROUP):
                value = grids[step, chunk, first + k, :, 0:LANES]
                state.append((value, zero_tile, roll(value, 2 * NZ), roll(value, 3 * NZ), zero_tile))
            for tile in range(tiles):
                columns = slice(tile * LANES, (tile + 1) * LANES)
                for k in range(GROUP):
                    here = first + k
                    value, two_before, two_here, one_after, one_before = state[k]
                    one_here = roll(value, NZ)
                    if tile < tiles - 1:
                        following = grids[step, chunk, here, :, (tile + 1) * LANES : (tile + 2) * LANES]
                        two_after, one_next = roll(following, 2 * NZ), roll(following, 3 * NZ)
                    else:
                        following, two_after, one_next = None, zero_tile, zero_tile
                    state[k] = (following, two_here, two_after, one_next, one_here)

                    def plane(shift):
                        return grids[step, chunk, here + shift, :, columns]

                    def cell(kind):
                        return cells[here, kind : kind + 1, columns]

                    total = cell(0) * value
                    total = total + cell(1) * (
                        (plane(-1) + plane(1)) - (plane(-2) + plane(2)) * RATIO
                    )
                    near = jnp.where(first_row, one_before, one_here) + jnp.where(
                        not_last, one_after, one_next
                    )
                    far = two_here + jnp.where(front_half, two_before, two_after)
                    total = total + cell(2) * (near - far * RATIO)
                    along = (back_one * roll(value, 1) + fore_one * roll(value, LANES - 1)) - (
                        back_two * roll(value, 2) + fore_two * roll(value, LANES - 2)
                    )
                    total = total + cell(3) * along
                    if step > 0:
                        total = total - grids[step - 1, chunk, here, :, columns]
                    else:
                        total = total * 0.5
                    results.append((here, columns, total))
            for here, columns, total in results:
                if step < DEGREE - 1:
                    grids[step + 1, chunk, here, :, columns] = total
                else:
                    last[chunk, here - planes, :, columns] = total
            return carry

        lax.fori_loop(0, (span - 2 * edge) // GROUP, some_planes, 0)

    def leave(chunk):
        rows = pl.ds(pl.multiple_of(band * held + side * half + chunk * TILE, TILE), TILE)
        for turn in range(bands):
            target = lax.rem(band + turn, bands)
            columns = pl.ds(pl.multiple_of(target * share, share), share)
            for other in (1, 0):
                source = last.at[chunk, slab(side if other == 0 else 1 - side), :, columns]
                landing = out.at[:, rows, :]
                if turn == 0 and other == 0:
                    pltpu.make_async_copy(source, landing, out_recv.at[0]).start()
                else:
                    pltpu.make_async_remote_copy(
                        src_ref=source,
                        dst_ref=landing,
                        send_sem=out_send.at[0],
                        recv_sem=out_recv.at[0],
                        device_id=to(target, space if other == 0 else partner),
                        device_id_type=MESH,
                    ).start()

    def finish(chunk):
        @pl.when(has_across)
        def _():
            halo_own[chunk].wait_recv()

        @pl.when(has_outward)
        def _():
            halo_passed[chunk].wait_recv()

        for step in range(DEGREE):
            apply(step, chunk)
        leave(chunk)

    for chunk in range(chunks):
        keep[chunk].wait()
        enter[chunk].wait_recv()

        @pl.when(has_across)
        def _():
            halo_passed[chunk].start()

        if chunk + 2 < chunks:
            begin(chunk + 2)
        if chunk > 0:
            finish(chunk - 1)
    finish(chunks - 1)

    for kind in range(2):
        base_sends[kind][0].wait_send()
    for chunk in range(chunks):
        enter[chunk].wait_send()

    @pl.when(has_outward)
    def _():
        for kind in range(2):
            base_sends[kind][1].wait_send()
        for chunk in range(chunks):
            halo_own[chunk].wait_send()

    @pl.when(has_across)
    def _():
        for kind in range(2):
            base_sends[kind][2].wait_send()
        for chunk in range(chunks):
            halo_passed[chunk].wait_send()

    pltpu.make_async_copy(out, out, out_recv.at[0]).wait()
    size = out.shape[1]
    middle = size // 2
    upper, lower = None, None
    for plane in range(planes):
        plane_high, plane_low = split(out[plane])
        high[plane], low[plane] = plane_high, plane_low
        both = (plane_high, plane_low)
        top = (plane_high[:middle], plane_low[:middle])
        bottom = (plane_high[middle:], plane_low[middle:])
        term = product(top, both, ((1,), (1,)))
        upper = term if upper is None else upper + term
        term = product(bottom, bottom, ((1,), (1,)))
        lower = term if lower is None else lower + term
    local[:middle, :] = upper
    local[middle:, middle:] = lower
    depth, arrived, settle = start_reduction(
        bands, spaces, cell_total, local, near, far, mine, final, gram, gram_send, gram_recv
    )
    for first in range(0, size, BLOCK):
        if first % depth == 0:
            arrived(first // depth)
        factor_rows(gram, pending, inverse, first, size)
    top = split(inverse[:middle, :middle])
    bottom = split(inverse[middle:, :])
    stores = []
    for plane in range(planes):
        staged[plane, :middle] = product(top, (high[plane, :middle], low[plane, :middle]), ((1,), (0,)))
        staged[plane, middle:] = product(bottom, (high[plane], low[plane]), ((1,), (0,)))
        stores.append(
            pltpu.make_async_copy(staged.at[plane], result.at[plane], store_sems.at[plane])
        )
        stores[-1].start()
    settle()
    for copy in stores:
        copy.wait()
    sent = out.at[:, 0 : out.shape[1] - out.shape[1] // (2 * bands), :]
    pltpu.make_async_copy(sent, sent, out_send.at[0]).wait()


def on_device(states, patch_ids, metric_table, potential):
    held, planes, plane_cells = states.shape
    bands = lax.axis_size("band")
    spaces = lax.axis_size("space")
    chunks = held // 2 // TILE
    total = held * bands
    depth = max(BLOCK, 2 * bands * TILE)
    pieces = total // depth
    share = depth // (2 * bands)
    if planes != REACH * DEGREE:
        raise ValueError("slab depth")
    dma = pltpu.SemaphoreType.DMA
    hbm = pl.BlockSpec(memory_space=pltpu.HBM)
    regrouped = (planes, total, plane_cells // bands)
    result = pl.pallas_call(
        functools.partial(filter_kernel, bands, spaces, float(planes * plane_cells * spaces)),
        out_shape=jax.ShapeDtypeStruct(regrouped, jnp.float32),
        in_specs=[hbm] * 4,
        out_specs=hbm,
        scratch_shapes=[
            pltpu.VMEM(regrouped, jnp.float32),
            pltpu.VMEM(regrouped, jnp.bfloat16),
            pltpu.VMEM(regrouped, jnp.bfloat16),
            pltpu.VMEM(regrouped, jnp.float32),
            pltpu.VMEM((total, total), jnp.float32),
            pltpu.VMEM((pieces, 2 * bands - 1, share, total), jnp.float32),
            pltpu.VMEM((pieces, spaces // 2, share, total), jnp.float32),
            pltpu.VMEM((pieces, share, total), jnp.float32),
            pltpu.VMEM((pieces, share, total), jnp.float32),
            pltpu.VMEM((total, total), jnp.float32),
            pltpu.VMEM((total, 2 * total), jnp.float32),
            pltpu.VMEM((total, total), jnp.float32),
            pltpu.VMEM((DEGREE, chunks, 4 * planes, TILE, plane_cells), jnp.float32),
            pltpu.VMEM((chunks, 2 * planes, TILE, plane_cells), jnp.float32),
            pltpu.VMEM((4 * planes, 4, plane_cells), jnp.float32),
            pltpu.VMEM((4,) + patch_ids.shape, jnp.int32),
            pltpu.VMEM((4,) + potential.shape, jnp.float32),
            pltpu.VMEM(metric_table.shape, jnp.float32),
            pltpu.VMEM((metric_table.shape[0], 3 * LANES), jnp.float32),
            dma((3,)),
            dma((2, 3)),
            dma((2, 3)),
            dma((chunks,)),
            dma((chunks,)),
            dma((chunks,)),
            dma((2, chunks)),
            dma((2, chunks)),
            dma((1,)),
            dma((1,)),
            dma((planes,)),
            dma((3, pieces)),
            dma((3, pieces)),
        ],
        compiler_params=pltpu.CompilerParams(
            collective_id=0, has_side_effects=True, vmem_limit_bytes=60 * 2**20
        ),
        name="orthonormal_states",
    )(states.transpose(1, 0, 2), patch_ids, metric_table, potential)
    return result.transpose(1, 0, 2)


def solution(mesh):
    return jax.shard_map(
        on_device,
        mesh=mesh,
        in_specs=(P("band", "space", None), P("space", None), P(), P("space", None)),
        out_specs=P(None, "space", "band"),
        check_vma=False,
    )
```

```python
import functools

import jax
import jax.numpy as jnp
from jax import lax
from jax.experimental import pallas as pl
from jax.experimental.pallas import tpu as pltpu
from jax.sharding import PartitionSpec as P

DEGREE = 3
NZ = 32


CENTRE = 8.5
HALF_WIDTH = 7.5
WEIGHTS = (-1.0 / 12.0, 4.0 / 3.0, -2.5, 4.0 / 3.0, -1.0 / 12.0)


MESH = pl.DeviceIdType.MESH
HIGHEST = lax.Precision.HIGHEST
BLOCK = 64
TILE = 8
STRIP = 16
LANES = 128


def matmul(left, right, dims):
    return lax.dot_general(
        left, right, (dims, ((), ())), precision=HIGHEST, preferred_element_type=jnp.float32
    )


def factor_block(diagonal):
    size = diagonal.shape[0]
    rows = lax.broadcasted_iota(jnp.int32, (size, size), 0)
    columns = lax.broadcasted_iota(jnp.int32, (size, size), 1)
    unit = jnp.where(rows == columns, 1.0, 0.0).astype(jnp.float32)
    rest = jnp.concatenate([diagonal, unit], axis=1)
    width = rest.shape[1]
    in_strip = lax.broadcasted_iota(jnp.int32, (STRIP, width), 0)
    done = []
    for start in range(0, size, STRIP):
        top, rest = rest[:STRIP], rest[STRIP:]
        panel = [
            jnp.broadcast_to(top[:, start + k : start + k + 1], top.shape) for k in range(STRIP)
        ]
        scale = jnp.zeros((STRIP, width), jnp.float32)
        for group in range(0, STRIP, TILE):
            weights, eliminated = {}, []
            for k in range(group, group + TILE):
                inverse = 1.0 / panel[k][k : k + 1, :]
                scale = jnp.where(in_strip == k, inverse, scale)
                below = jnp.where(in_strip > k, panel[k], 0.0)
                row = top[k : k + 1, :] * inverse
                for later in range(k + 1, STRIP):
                    weights[k, later] = panel[later][k : k + 1, :] * inverse
                    panel[later] = panel[later] - below * weights[k, later]
                top = top - below * row
                eliminated.append(row)
            if size - start > STRIP:
                columns_of = [
                    jnp.broadcast_to(rest[:, start + k : start + k + 1], rest.shape)
                    for k in range(group, group + TILE)
                ]
                total = None
                for k in range(TILE):
                    for later in range(k + 1, TILE):
                        columns_of[later] = (
                            columns_of[later] - columns_of[k] * weights[group + k, group + later]
                        )
                    term = columns_of[k] * eliminated[k]
                    total = term if total is None else total + term
                rest = rest - total
        done.append(top * jnp.sqrt(scale))
    return jnp.concatenate(done, axis=0)[:, size:]


def start_factor(pending, size):
    rows = lax.broadcasted_iota(jnp.int32, (size, 2 * size), 0)
    columns = lax.broadcasted_iota(jnp.int32, (size, 2 * size), 1)
    pending[...] = jnp.where(columns == rows + size, 1.0, 0.0).astype(jnp.float32)


def factor_rows(gram_rows, pending, inverse, first, size):
    last = first + BLOCK
    low = first // LANES * LANES
    high = size + -(-last // LANES) * LANES
    current = jnp.concatenate(
        [
            gram_rows + pending[first:last, low:size],
            pending[first:last, size:high],
        ],
        axis=1,
    )
    small = factor_block(current[:, first - low : last - low])
    rows = matmul(small, current, ((1,), (0,)))
    inverse[first:last, 0 : high - size] = rows[:, size - low :]
    if last < size:
        aligned = last // LANES * LANES
        update = matmul(rows[:, aligned - low : size - low], rows, ((0,), (0,)))
        pending[last:, low:high] -= update[last - aligned :]


def start_reduction(bands, spaces, cell_total, local, near, far, mine, final, gram, send_sems, recv_sems):
    size = local.shape[0]
    near_count, far_count = 2 * bands, spaces // 2
    pieces, share = near.shape[0], near.shape[2]
    depth = share * near_count
    band, space = lax.axis_index("band"), lax.axis_index("space")
    line = space // 2
    side = space - 2 * line
    place = 2 * band + side

    def rows_of(piece, index):
        return pl.ds(pl.multiple_of(piece * depth + index * share, share), share)

    def columns_of(piece):
        return slice(piece * depth // LANES * LANES, size)

    def near_peer(offset):
        index = lax.rem(place + offset, near_count)
        return index, {"band": index // 2, "space": 2 * line + lax.rem(index, 2)}

    def far_peer(offset):
        return {"band": band, "space": 2 * lax.rem(line + offset, far_count) + side}

    def send(source, landing, stage, piece, target):
        pltpu.make_async_remote_copy(
            src_ref=source,
            dst_ref=landing,
            send_sem=send_sems.at[stage, piece],
            recv_sem=recv_sems.at[stage, piece],
            device_id=target,
            device_id_type=MESH,
        ).start()

    def bytes_of(stage, piece):
        columns = columns_of(piece)
        if stage == 1:
            return far.at[piece, 0 : far_count - 1, :, columns]
        return near.at[piece, :, :, columns]

    def wait(sems, stage, piece):
        moved = bytes_of(stage, piece)
        pltpu.make_async_copy(moved, moved, sems.at[stage, piece]).wait()

    def begin(piece):
        columns = columns_of(piece)
        for offset in range(1, near_count):
            index, target = near_peer(offset)
            send(
                local.at[rows_of(piece, index), columns], near.at[piece, offset - 1, :, columns],
                0, piece, target,
            )

    def relay():
        for piece in range(pieces):
            columns = columns_of(piece)
            wait(recv_sems, 0, piece)
            mine[piece, :, columns] = (
                jnp.sum(near[piece, :, :, columns], axis=0) + local[rows_of(piece, place), columns]
            )
            for offset in range(1, far_count):
                send(
                    mine.at[piece, :, columns], far.at[piece, line, :, columns], 1, piece,
                    far_peer(offset),
                )
        for piece in range(pieces):
            columns = columns_of(piece)
            wait(recv_sems, 1, piece)
            far[piece, line, :, columns] = mine[piece, :, columns]
            final[piece, :, columns] = jnp.sum(far[piece, :, :, columns], axis=0) / cell_total
            for offset in range(1, near_count):
                send(
                    final.at[piece, :, columns], gram.at[rows_of(piece, place), columns], 2, piece,
                    near_peer(offset)[1],
                )

    def arrived(piece):
        columns = columns_of(piece)
        wait(recv_sems, 2, piece)
        gram[rows_of(piece, place), columns] = final[piece, :, columns]

    def settle():
        for stage in range(3):
            for piece in range(pieces):
                wait(send_sems, stage, piece)

    return begin, relay, arrived, settle


FIRST = 4.0 / 3.0
RATIO = 1.0 / 16.0
REACH = 2
GROUP = 4


def split(value):
    high = value.astype(jnp.bfloat16)
    return high, (value - high.astype(jnp.float32)).astype(jnp.bfloat16)


def product(left, right, dims):
    left_high, left_low = left
    right_high, right_low = right

    def one(first, second):
        return lax.dot_general(first, second, (dims, ((), ())), preferred_element_type=jnp.float32)

    return one(left_high, right_high) + (one(left_high, right_low) + one(left_low, right_high))


def filter_kernel(
    bands, spaces, cell_total, states, ids, table_in, potential, result, out, high, low, staged,
    local, near, far, mine, final, gram, pending, inverse, grids, last, cells, near_ids, near_pot,
    table, tables, first_sems, base_send, base_recv, in_send, in_recv, keep_sems, halo_send, halo_recv, out_send,
    out_recv, store_sems, gram_send, gram_recv,
):
    planes, held, plane_cells = states.shape
    half = held // 2
    chunks = half // TILE
    span = 4 * planes
    share = plane_cells // bands
    tiles = plane_cells // LANES
    band = lax.axis_index("band")
    space = lax.axis_index("space")
    side = lax.rem(space, 2)
    partner = space + 1 - 2 * side
    outward = space + 4 * side - 2
    across = space - 4 * side + 2
    has_outward = jnp.logical_and(outward >= 0, outward < spaces)
    has_across = jnp.logical_and(across >= 0, across < spaces)

    def to(target_band, target_space):
        return {"band": target_band, "space": target_space}

    own, theirs = 1 + side, 2 - side
    firsts = [
        pltpu.make_async_copy(source, landing, first_sems.at[number])
        for number, (source, landing) in enumerate(
            ((ids, near_ids.at[own]), (potential, near_pot.at[own]), (table_in, table))
        )
    ]
    for copy in firsts:
        copy.start()

    barrier = pltpu.get_barrier_semaphore()
    for turn in range(bands):
        target = lax.rem(band + turn, bands)
        if turn:
            pl.semaphore_signal(
                barrier, inc=1, device_id=to(target, space), device_id_type=MESH
            )
        pl.semaphore_signal(barrier, inc=1, device_id=to(target, partner), device_id_type=MESH)
    lines = spaces // 2
    for offset in range(1, lines):
        pl.semaphore_signal(
            barrier,
            inc=1,
            device_id=to(band, 2 * lax.rem(space // 2 + offset, lines) + side),
            device_id_type=MESH,
        )
    pl.semaphore_wait(barrier, 2 * bands + lines - 2)

    def slab(place):
        return pl.ds(place * planes, planes)

    def rows_of(part, chunk):
        return pl.ds(pl.multiple_of(part * half + chunk * TILE, TILE), TILE)

    def remote(source, landing, send_sem, recv_sem, target):
        return pltpu.make_async_remote_copy(
            src_ref=source,
            dst_ref=landing,
            send_sem=send_sem,
            recv_sem=recv_sem,
            device_id=to(band, target),
            device_id_type=MESH,
        )

    own_landing, passed_landing = 3 * (1 - side), 3 * side
    base_sends = []
    for kind, (source, landing) in enumerate(((ids, near_ids), (potential, near_pot))):
        base_sends.append(
            (
                remote(source, landing.at[own], base_send.at[kind, 0], base_recv.at[kind, 0], partner),
                remote(source, landing.at[own_landing], base_send.at[kind, 1], base_recv.at[kind, 1], outward),
                remote(
                    landing.at[theirs], landing.at[passed_landing],
                    base_send.at[kind, 2], base_recv.at[kind, 2], across,
                ),
            )
        )
    enter, keep, halo_own, halo_passed = [], [], [], []
    for chunk in range(chunks):
        grid = grids.at[0, chunk]
        kept = states.at[:, rows_of(side, chunk)]
        enter.append(
            remote(
                states.at[:, rows_of(1 - side, chunk)], grid.at[slab(own)],
                in_send.at[chunk], in_recv.at[chunk], partner,
            )
        )
        keep.append(pltpu.make_async_copy(kept, grid.at[slab(own)], keep_sems.at[chunk]))
        halo_own.append(
            remote(
                kept, grid.at[slab(own_landing)],
                halo_send.at[0, chunk], halo_recv.at[0, chunk], outward,
            )
        )
        halo_passed.append(
            remote(
                grid.at[slab(theirs)], grid.at[slab(passed_landing)],
                halo_send.at[1, chunk], halo_recv.at[1, chunk], across,
            )
        )

    def begin(chunk):
        enter[chunk].start()

        @pl.when(has_outward)
        def _():
            halo_own[chunk].start()

    for kind in range(2):
        base_sends[kind][0].start()

    @pl.when(has_outward)
    def _():
        for kind in range(2):
            base_sends[kind][1].start()

    for chunk in range(min(2, chunks)):
        begin(chunk)
    for chunk in range(chunks):
        keep[chunk].start()
    for copy in firsts:
        copy.wait()
    missing_places = ((0, space < 2), (3, space >= spaces - 2))
    for place, missing in missing_places:

        @pl.when(missing)
        def _():
            near_ids[place] = jnp.zeros(near_ids.shape[1:], jnp.int32)
            near_pot[place] = jnp.zeros(near_pot.shape[1:], jnp.float32)
            for chunk in range(chunks):
                for plane in range(place * planes, (place + 1) * planes):
                    grids[0, chunk, plane] = jnp.zeros((TILE, plane_cells), jnp.float32)

    patches = table.shape[0]
    depth = table.shape[1] // 3
    source = lax.broadcasted_iota(jnp.int32, (table.shape[1], 3 * LANES), 0)
    lane_of = lax.broadcasted_iota(jnp.int32, (table.shape[1], 3 * LANES), 1)
    wanted = lane_of // LANES * depth + lane_of % depth
    spread = jnp.where(source == wanted, 1.0, 0.0).astype(jnp.float32)
    tables[...] = matmul(table[...], spread, ((1,), (0,)))

    for kind in range(2):
        base_sends[kind][0].wait_recv()

    @pl.when(has_across)
    def _():
        for kind in range(2):
            base_sends[kind][2].start()
        for kind in range(2):
            base_sends[kind][1].wait_recv()

    @pl.when(has_outward)
    def _():
        for kind in range(2):
            base_sends[kind][2].wait_recv()

    row_source = lax.broadcasted_iota(jnp.int32, (ids.shape[1], plane_cells), 0)
    row_lane = lax.broadcasted_iota(jnp.int32, (ids.shape[1], plane_cells), 1)
    row_spread = jnp.where(row_source == row_lane // NZ, 1.0, 0.0).astype(jnp.float32)

    def make_cells(place, carry):
        patch = matmul(near_ids[place].astype(jnp.float32), row_spread, ((1,), (0,)))
        zero = jnp.zeros(patch.shape, jnp.float32)

        def look(step, metric):
            rows = tables[pl.ds(pl.multiple_of(TILE * step, TILE), TILE), :]
            for row in range(TILE):
                here = patch == (TILE * step + row).astype(jnp.float32)
                metric = tuple(
                    jnp.where(
                        here,
                        jnp.concatenate(
                            [rows[row : row + 1, kind * LANES : (kind + 1) * LANES]] * tiles, axis=1
                        ),
                        value,
                    )
                    for kind, value in enumerate(metric)
                )
            return metric

        metric = lax.fori_loop(0, patches // TILE, look, (zero, zero, zero))
        kinetic = [value * (-1.0 / HALF_WIDTH) for value in metric]
        centre = (near_pot[place] - CENTRE) * (2.0 / HALF_WIDTH) + WEIGHTS[2] * (
            kinetic[0] + kinetic[1] + kinetic[2]
        )
        for kind, value in enumerate([centre] + [FIRST * value for value in kinetic]):
            for plane in range(planes):
                cells[place * planes + plane, kind : kind + 1] = value[plane : plane + 1]
        return carry

    lax.fori_loop(0, 4, make_cells, 0)
    for place, missing in missing_places:

        @pl.when(missing)
        def _():
            for plane in range(place * planes, (place + 1) * planes):
                cells[plane] = jnp.zeros(cells.shape[1:], jnp.float32)

    start_factor(pending, pending.shape[0])
    lane = lax.broadcasted_iota(jnp.int32, (TILE, LANES), 1)
    depth_at = lane % NZ
    zero_tile = jnp.zeros((TILE, LANES), jnp.float32)

    def mask(inside, weight):
        return jnp.where(inside, weight, 0.0).astype(jnp.float32)

    back_one, fore_one = mask(depth_at >= 1, 1.0), mask(depth_at < NZ - 1, 1.0)
    back_two, fore_two = mask(depth_at >= 2, RATIO), mask(depth_at < NZ - 2, RATIO)
    first_row, front_half, not_last = lane < NZ, lane < 2 * NZ, lane < 3 * NZ

    def roll(value, amount):
        return pltpu.roll(value, amount, axis=1)

    def apply(step, chunk):
        edge = REACH * (step + 1)

        def some_planes(number, carry):
            first = edge + GROUP * number
            results = []
            state = []
            for k in range(GROUP):
                value = grids[step, chunk, first + k, :, 0:LANES]
                state.append((value, zero_tile, roll(value, 2 * NZ), roll(value, 3 * NZ), zero_tile))
            for tile in range(tiles):
                columns = slice(tile * LANES, (tile + 1) * LANES)
                for k in range(GROUP):
                    here = first + k
                    value, two_before, two_here, one_after, one_before = state[k]
                    one_here = roll(value, NZ)
                    if tile < tiles - 1:
                        following = grids[step, chunk, here, :, (tile + 1) * LANES : (tile + 2) * LANES]
                        two_after, one_next = roll(following, 2 * NZ), roll(following, 3 * NZ)
                    else:
                        following, two_after, one_next = None, zero_tile, zero_tile
                    state[k] = (following, two_here, two_after, one_next, one_here)

                    def plane(shift):
                        return grids[step, chunk, here + shift, :, columns]

                    def cell(kind):
                        return cells[here, kind : kind + 1, columns]

                    total = cell(0) * value
                    total = total + cell(1) * (
                        (plane(-1) + plane(1)) - (plane(-2) + plane(2)) * RATIO
                    )
                    near = jnp.where(first_row, one_before, one_here) + jnp.where(
                        not_last, one_after, one_next
                    )
                    far = two_here + jnp.where(front_half, two_before, two_after)
                    total = total + cell(2) * (near - far * RATIO)
                    along = (back_one * roll(value, 1) + fore_one * roll(value, LANES - 1)) - (
                        back_two * roll(value, 2) + fore_two * roll(value, LANES - 2)
                    )
                    total = total + cell(3) * along
                    if step > 0:
                        total = total - grids[step - 1, chunk, here, :, columns]
                    else:
                        total = total * 0.5
                    results.append((here, columns, total))
            for here, columns, total in results:
                if step < DEGREE - 1:
                    grids[step + 1, chunk, here, :, columns] = total
                else:
                    last[chunk, here - planes, :, columns] = total
            return carry

        lax.fori_loop(0, (span - 2 * edge) // GROUP, some_planes, 0)

    def leave(chunk):
        rows = pl.ds(pl.multiple_of(band * held + side * half + chunk * TILE, TILE), TILE)
        for turn in range(bands):
            target = lax.rem(band + turn, bands)
            columns = pl.ds(pl.multiple_of(target * share, share), share)
            for other in (1, 0):
                source = last.at[chunk, slab(side if other == 0 else 1 - side), :, columns]
                landing = out.at[:, rows, :]
                if turn == 0 and other == 0:
                    pltpu.make_async_copy(source, landing, out_recv.at[0]).start()
                else:
                    pltpu.make_async_remote_copy(
                        src_ref=source,
                        dst_ref=landing,
                        send_sem=out_send.at[0],
                        recv_sem=out_recv.at[0],
                        device_id=to(target, space if other == 0 else partner),
                        device_id_type=MESH,
                    ).start()

    def finish(chunk):
        @pl.when(has_across)
        def _():
            halo_own[chunk].wait_recv()

        @pl.when(has_outward)
        def _():
            halo_passed[chunk].wait_recv()

        for step in range(DEGREE):
            apply(step, chunk)
        leave(chunk)

    for chunk in range(chunks):
        keep[chunk].wait()
        enter[chunk].wait_recv()

        @pl.when(has_across)
        def _():
            halo_passed[chunk].start()

        if chunk + 2 < chunks:
            begin(chunk + 2)
        if chunk > 0:
            finish(chunk - 1)
    finish(chunks - 1)

    for kind in range(2):
        base_sends[kind][0].wait_send()
    for chunk in range(chunks):
        enter[chunk].wait_send()

    @pl.when(has_outward)
    def _():
        for kind in range(2):
            base_sends[kind][1].wait_send()
        for chunk in range(chunks):
            halo_own[chunk].wait_send()

    @pl.when(has_across)
    def _():
        for kind in range(2):
            base_sends[kind][2].wait_send()
        for chunk in range(chunks):
            halo_passed[chunk].wait_send()

    pltpu.make_async_copy(out, out, out_recv.at[0]).wait()
    size = out.shape[1]
    middle = size // 2
    for plane in range(planes):
        high[plane], low[plane] = split(out[plane])

    def gram_of(first, last):
        begin = first // LANES * LANES
        sums = None
        for plane in range(planes):
            term = product(
                (high[plane, first:last], low[plane, first:last]),
                (high[plane, begin:], low[plane, begin:]),
                ((1,), (1,)),
            )
            sums = term if sums is None else sums + term
        return sums

    begin, relay, arrived, settle = start_reduction(
        bands, spaces, cell_total, local, near, far, mine, final, gram, gram_send, gram_recv
    )
    pieces = near.shape[0]
    depth = near.shape[2] * 2 * bands
    folded = pieces * depth < size
    first_rows = gram_of(0, 2 * depth if folded else depth)
    local[:depth] = first_rows[:depth]
    begin(0)
    if folded:
        in_front = lax.broadcasted_iota(jnp.int32, (depth, LANES), 1) < depth
        second = first_rows[depth:]
        both = gram_of(2 * depth, 4 * depth)
        local[depth : 2 * depth, :LANES] = jnp.where(
            in_front, pltpu.roll(both[depth:], depth, axis=1), second[:, :LANES]
        )
        local[depth : 2 * depth, LANES:] = second[:, LANES:]
        local[2 * depth : 3 * depth, middle:] = both[:depth]
    else:
        for piece in range(1, pieces):
            local[piece * depth : (piece + 1) * depth, piece * depth // LANES * LANES :] = gram_of(
                piece * depth, (piece + 1) * depth
            )
    for piece in range(1, pieces):
        begin(piece)
    relay()
    for first in range(0, size, BLOCK):
        piece = first // depth
        if first % depth == 0 and piece < pieces:
            arrived(piece)
        if piece < pieces:
            rows = gram[first : first + BLOCK, first // LANES * LANES :]
        else:
            rows = pltpu.roll(gram[depth : 2 * depth, :LANES], depth, axis=1)
        factor_rows(rows, pending, inverse, first, size)
    top = split(inverse[:middle, :middle])
    bottom = split(inverse[middle:, :])
    stores = []
    for plane in range(planes):
        staged[plane, :middle] = product(top, (high[plane, :middle], low[plane, :middle]), ((1,), (0,)))
        staged[plane, middle:] = product(bottom, (high[plane], low[plane]), ((1,), (0,)))
        stores.append(
            pltpu.make_async_copy(staged.at[plane], result.at[plane], store_sems.at[plane])
        )
        stores[-1].start()
    settle()
    for copy in stores:
        copy.wait()
    sent = out.at[:, 0 : out.shape[1] - out.shape[1] // (2 * bands), :]
    pltpu.make_async_copy(sent, sent, out_send.at[0]).wait()


def hand_over_kernel(source, result, held, load_sems, store_sems):
    parts = [
        (plane, pl.ds(first, LANES))
        for plane in range(source.shape[0])
        for first in range(0, source.shape[1], LANES)
    ]
    loads = [
        pltpu.make_async_copy(source.at[part], held.at[part], load_sems.at[number])
        for number, part in enumerate(parts)
    ]
    stores = [
        pltpu.make_async_copy(held.at[part], result.at[part], store_sems.at[number])
        for number, part in enumerate(parts)
    ]
    for load in loads:
        load.start()
    for load, store in zip(loads, stores):
        load.wait()
        store.start()
    for store in stores:
        store.wait()


def handed_over(values):
    hbm = pl.BlockSpec(memory_space=pltpu.HBM)
    count = values.shape[0] * (values.shape[1] // LANES)
    return pl.pallas_call(
        hand_over_kernel,
        out_shape=jax.ShapeDtypeStruct(values.shape, values.dtype),
        in_specs=[hbm],
        out_specs=hbm,
        scratch_shapes=[
            pltpu.VMEM(values.shape, values.dtype),
            pltpu.SemaphoreType.DMA((count,)),
            pltpu.SemaphoreType.DMA((count,)),
        ],
        compiler_params=pltpu.CompilerParams(vmem_limit_bytes=60 * 2**20),
        name="hand_over",
    )(values)


def on_device(states, patch_ids, metric_table, potential):
    held, planes, plane_cells = states.shape
    bands = lax.axis_size("band")
    spaces = lax.axis_size("space")
    chunks = held // 2 // TILE
    total = held * bands
    depth = max(BLOCK, 2 * bands * TILE)
    folded = depth == BLOCK and total == 4 * BLOCK and LANES == 2 * BLOCK
    pieces = total // depth - int(folded)
    share = depth // (2 * bands)
    if planes != REACH * DEGREE:
        raise ValueError("slab depth")
    dma = pltpu.SemaphoreType.DMA
    hbm = pl.BlockSpec(memory_space=pltpu.HBM)
    regrouped = (planes, total, plane_cells // bands)
    result = pl.pallas_call(
        functools.partial(filter_kernel, bands, spaces, float(planes * plane_cells * spaces)),
        out_shape=jax.ShapeDtypeStruct(regrouped, jnp.float32),
        in_specs=[hbm] * 4,
        out_specs=hbm,
        scratch_shapes=[
            pltpu.VMEM(regrouped, jnp.float32),
            pltpu.VMEM(regrouped, jnp.bfloat16),
            pltpu.VMEM(regrouped, jnp.bfloat16),
            pltpu.VMEM(regrouped, jnp.float32),
            pltpu.VMEM((total, total), jnp.float32),
            pltpu.VMEM((pieces, 2 * bands - 1, share, total), jnp.float32),
            pltpu.VMEM((pieces, spaces // 2, share, total), jnp.float32),
            pltpu.VMEM((pieces, share, total), jnp.float32),
            pltpu.VMEM((pieces, share, total), jnp.float32),
            pltpu.VMEM((total, total), jnp.float32),
            pltpu.VMEM((total, 2 * total), jnp.float32),
            pltpu.VMEM((total, total), jnp.float32),
            pltpu.VMEM((DEGREE, chunks, 4 * planes, TILE, plane_cells), jnp.float32),
            pltpu.VMEM((chunks, 2 * planes, TILE, plane_cells), jnp.float32),
            pltpu.VMEM((4 * planes, 4, plane_cells), jnp.float32),
            pltpu.VMEM((4,) + patch_ids.shape, jnp.int32),
            pltpu.VMEM((4,) + potential.shape, jnp.float32),
            pltpu.VMEM(metric_table.shape, jnp.float32),
            pltpu.VMEM((metric_table.shape[0], 3 * LANES), jnp.float32),
            dma((3,)),
            dma((2, 3)),
            dma((2, 3)),
            dma((chunks,)),
            dma((chunks,)),
            dma((chunks,)),
            dma((2, chunks)),
            dma((2, chunks)),
            dma((1,)),
            dma((1,)),
            dma((planes,)),
            dma((3, pieces)),
            dma((3, pieces)),
        ],
        compiler_params=pltpu.CompilerParams(
            collective_id=0, has_side_effects=True, vmem_limit_bytes=60 * 2**20
        ),
        name="orthonormal_states",
    )(states.transpose(1, 0, 2), patch_ids, metric_table, potential)
    return handed_over(result).transpose(1, 0, 2)


def solution(mesh):
    return jax.shard_map(
        on_device,
        mesh=mesh,
        in_specs=(P("band", "space", None), P("space", None), P(), P("space", None)),
        out_specs=P(None, "space", "band"),
        check_vma=False,
    )
```

```python
import functools

import jax
import jax.numpy as jnp
from jax import lax
from jax.experimental import pallas as pl
from jax.experimental.pallas import tpu as pltpu
from jax.sharding import PartitionSpec as P

DEGREE = 3
NZ = 32


CENTRE = 8.5
HALF_WIDTH = 7.5
WEIGHTS = (-1.0 / 12.0, 4.0 / 3.0, -2.5, 4.0 / 3.0, -1.0 / 12.0)


MESH = pl.DeviceIdType.MESH
HIGHEST = lax.Precision.HIGHEST
BLOCK = 64
TILE = 8
STRIP = 16
LANES = 128


def matmul(left, right, dims):
    return lax.dot_general(
        left, right, (dims, ((), ())), precision=HIGHEST, preferred_element_type=jnp.float32
    )


def factor_block(diagonal):
    size = diagonal.shape[0]
    rows = lax.broadcasted_iota(jnp.int32, (size, size), 0)
    columns = lax.broadcasted_iota(jnp.int32, (size, size), 1)
    unit = jnp.where(rows == columns, 1.0, 0.0).astype(jnp.float32)
    rest = jnp.concatenate([diagonal, unit], axis=1)
    width = rest.shape[1]
    in_strip = lax.broadcasted_iota(jnp.int32, (STRIP, width), 0)
    done = []
    for start in range(0, size, STRIP):
        top, rest = rest[:STRIP], rest[STRIP:]
        panel = [
            jnp.broadcast_to(top[:, start + k : start + k + 1], top.shape) for k in range(STRIP)
        ]
        scale = jnp.zeros((STRIP, width), jnp.float32)
        for group in range(0, STRIP, TILE):
            weights, eliminated = {}, []
            for k in range(group, group + TILE):
                inverse = 1.0 / panel[k][k : k + 1, :]
                scale = jnp.where(in_strip == k, inverse, scale)
                below = jnp.where(in_strip > k, panel[k], 0.0)
                row = top[k : k + 1, :] * inverse
                for later in range(k + 1, STRIP):
                    weights[k, later] = panel[later][k : k + 1, :] * inverse
                    panel[later] = panel[later] - below * weights[k, later]
                top = top - below * row
                eliminated.append(row)
            if size - start > STRIP:
                columns_of = [
                    jnp.broadcast_to(rest[:, start + k : start + k + 1], rest.shape)
                    for k in range(group, group + TILE)
                ]
                total = None
                for k in range(TILE):
                    for later in range(k + 1, TILE):
                        columns_of[later] = (
                            columns_of[later] - columns_of[k] * weights[group + k, group + later]
                        )
                    term = columns_of[k] * eliminated[k]
                    total = term if total is None else total + term
                rest = rest - total
        done.append(top * jnp.sqrt(scale))
    return jnp.concatenate(done, axis=0)[:, size:]


def start_factor(pending, size):
    rows = lax.broadcasted_iota(jnp.int32, (size, 2 * size), 0)
    columns = lax.broadcasted_iota(jnp.int32, (size, 2 * size), 1)
    pending[...] = jnp.where(columns == rows + size, 1.0, 0.0).astype(jnp.float32)


def factor_rows(gram_rows, pending, inverse, first, size):
    last = first + BLOCK
    low = first // LANES * LANES
    high = size + -(-last // LANES) * LANES
    current = jnp.concatenate(
        [
            gram_rows + pending[first:last, low:size],
            pending[first:last, size:high],
        ],
        axis=1,
    )
    small = factor_block(current[:, first - low : last - low])
    rows = matmul(small, current, ((1,), (0,)))
    inverse[first:last, 0 : high - size] = rows[:, size - low :]
    if last < size:
        aligned = last // LANES * LANES
        update = matmul(rows[:, aligned - low : size - low], rows, ((0,), (0,)))
        pending[last:, low:high] -= update[last - aligned :]


def start_reduction(bands, spaces, cell_total, local, near, far, mine, final, gram, send_sems, recv_sems):
    size = local.shape[0]
    near_count, far_count = 2 * bands, spaces // 2
    pieces, share = near.shape[0], near.shape[2]
    depth = share * near_count
    band, space = lax.axis_index("band"), lax.axis_index("space")
    line = space // 2
    side = space - 2 * line
    place = 2 * band + side

    def rows_of(piece, index):
        return pl.ds(pl.multiple_of(piece * depth + index * share, share), share)

    def columns_of(piece):
        return slice(piece * depth // LANES * LANES, size)

    def near_peer(offset):
        index = lax.rem(place + offset, near_count)
        return index, {"band": index // 2, "space": 2 * line + lax.rem(index, 2)}

    def far_peer(offset):
        return {"band": band, "space": 2 * lax.rem(line + offset, far_count) + side}

    def send(source, landing, stage, piece, target):
        pltpu.make_async_remote_copy(
            src_ref=source,
            dst_ref=landing,
            send_sem=send_sems.at[stage, piece],
            recv_sem=recv_sems.at[stage, piece],
            device_id=target,
            device_id_type=MESH,
        ).start()

    def bytes_of(stage, piece):
        columns = columns_of(piece)
        if stage == 1:
            return far.at[piece, 0 : far_count - 1, :, columns]
        return near.at[piece, :, :, columns]

    def wait(sems, stage, piece):
        moved = bytes_of(stage, piece)
        pltpu.make_async_copy(moved, moved, sems.at[stage, piece]).wait()

    def begin(piece):
        columns = columns_of(piece)
        for offset in range(1, near_count):
            index, target = near_peer(offset)
            send(
                local.at[rows_of(piece, index), columns], near.at[piece, offset - 1, :, columns],
                0, piece, target,
            )

    def relay():
        for piece in range(pieces):
            columns = columns_of(piece)
            wait(recv_sems, 0, piece)
            mine[piece, :, columns] = (
                jnp.sum(near[piece, :, :, columns], axis=0) + local[rows_of(piece, place), columns]
            )
            for offset in range(1, far_count):
                send(
                    mine.at[piece, :, columns], far.at[piece, line, :, columns], 1, piece,
                    far_peer(offset),
                )
        for piece in range(pieces):
            columns = columns_of(piece)
            wait(recv_sems, 1, piece)
            far[piece, line, :, columns] = mine[piece, :, columns]
            final[piece, :, columns] = jnp.sum(far[piece, :, :, columns], axis=0) / cell_total
            for offset in range(1, near_count):
                send(
                    final.at[piece, :, columns], gram.at[rows_of(piece, place), columns], 2, piece,
                    near_peer(offset)[1],
                )

    def arrived(piece):
        columns = columns_of(piece)
        wait(recv_sems, 2, piece)
        gram[rows_of(piece, place), columns] = final[piece, :, columns]

    def settle():
        for stage in range(3):
            for piece in range(pieces):
                wait(send_sems, stage, piece)

    return begin, relay, arrived, settle


FIRST = 4.0 / 3.0
RATIO = 1.0 / 16.0
REACH = 2
GROUP = 4


def split(value):
    high = value.astype(jnp.bfloat16)
    return high, (value - high.astype(jnp.float32)).astype(jnp.bfloat16)


def product(left, right, dims):
    left_high, left_low = left
    right_high, right_low = right

    def one(first, second):
        return lax.dot_general(first, second, (dims, ((), ())), preferred_element_type=jnp.float32)

    return one(left_high, right_high) + (one(left_high, right_low) + one(left_low, right_high))


def filter_kernel(
    bands, spaces, cell_total, states, packed, result, out, high, low, staged,
    local, near, far, mine, final, gram, pending, inverse, grids, last, cells, near_ids, near_pot,
    tables, base_send, base_recv, in_send, in_recv, keep_sems, halo_send, halo_recv, out_send,
    out_recv, store_sems, gram_send, gram_recv,
):
    planes, held, plane_cells = states.shape
    half = held // 2
    chunks = half // TILE
    span = 4 * planes
    share = plane_cells // bands
    tiles = plane_cells // LANES
    band = lax.axis_index("band")
    space = lax.axis_index("space")
    side = lax.rem(space, 2)
    partner = space + 1 - 2 * side
    outward = space + 4 * side - 2
    across = space - 4 * side + 2
    has_outward = jnp.logical_and(outward >= 0, outward < spaces)
    has_across = jnp.logical_and(across >= 0, across < spaces)

    def to(target_band, target_space):
        return {"band": target_band, "space": target_space}

    own, theirs = 1 + side, 2 - side
    potential = packed.at[0:TILE]
    ids = packed.at[TILE : 2 * TILE, 0:LANES]
    table = packed[2 * TILE :, 0:LANES]

    barrier = pltpu.get_barrier_semaphore()
    for turn in range(bands):
        target = lax.rem(band + turn, bands)
        if turn:
            pl.semaphore_signal(
                barrier, inc=1, device_id=to(target, space), device_id_type=MESH
            )
        pl.semaphore_signal(barrier, inc=1, device_id=to(target, partner), device_id_type=MESH)
    lines = spaces // 2
    for offset in range(1, lines):
        pl.semaphore_signal(
            barrier,
            inc=1,
            device_id=to(band, 2 * lax.rem(space // 2 + offset, lines) + side),
            device_id_type=MESH,
        )
    pl.semaphore_wait(barrier, 2 * bands + lines - 2)

    def slab(place):
        return pl.ds(place * planes, planes)

    def rows_of(part, chunk):
        return pl.ds(pl.multiple_of(part * half + chunk * TILE, TILE), TILE)

    def remote(source, landing, send_sem, recv_sem, target):
        return pltpu.make_async_remote_copy(
            src_ref=source,
            dst_ref=landing,
            send_sem=send_sem,
            recv_sem=recv_sem,
            device_id=to(band, target),
            device_id_type=MESH,
        )

    own_landing, passed_landing = 3 * (1 - side), 3 * side
    base_sends = []
    for kind, (source, landing) in enumerate(((ids, near_ids), (potential, near_pot))):
        base_sends.append(
            (
                remote(source, landing.at[own], base_send.at[kind, 0], base_recv.at[kind, 0], partner),
                remote(source, landing.at[own_landing], base_send.at[kind, 1], base_recv.at[kind, 1], outward),
                remote(
                    landing.at[theirs], landing.at[passed_landing],
                    base_send.at[kind, 2], base_recv.at[kind, 2], across,
                ),
            )
        )
    enter, keep, halo_own, halo_passed = [], [], [], []
    for chunk in range(chunks):
        grid = grids.at[0, chunk]
        kept = states.at[:, rows_of(side, chunk)]
        enter.append(
            remote(
                states.at[:, rows_of(1 - side, chunk)], grid.at[slab(own)],
                in_send.at[chunk], in_recv.at[chunk], partner,
            )
        )
        keep.append(pltpu.make_async_copy(kept, grid.at[slab(own)], keep_sems.at[chunk]))
        halo_own.append(
            remote(
                kept, grid.at[slab(own_landing)],
                halo_send.at[0, chunk], halo_recv.at[0, chunk], outward,
            )
        )
        halo_passed.append(
            remote(
                grid.at[slab(theirs)], grid.at[slab(passed_landing)],
                halo_send.at[1, chunk], halo_recv.at[1, chunk], across,
            )
        )

    def begin(chunk):
        enter[chunk].start()

        @pl.when(has_outward)
        def _():
            halo_own[chunk].start()

    for kind in range(2):
        base_sends[kind][0].start()

    @pl.when(has_outward)
    def _():
        for kind in range(2):
            base_sends[kind][1].start()

    for chunk in range(min(2, chunks)):
        begin(chunk)
    for chunk in range(chunks):
        keep[chunk].start()
    near_ids[own] = ids[...]
    near_pot[own] = potential[...]
    missing_places = ((0, space < 2), (3, space >= spaces - 2))
    for place, missing in missing_places:

        @pl.when(missing)
        def _():
            near_ids[place] = jnp.zeros(near_ids.shape[1:], jnp.float32)
            near_pot[place] = jnp.zeros(near_pot.shape[1:], jnp.float32)
            for chunk in range(chunks):
                for plane in range(place * planes, (place + 1) * planes):
                    grids[0, chunk, plane] = jnp.zeros((TILE, plane_cells), jnp.float32)

    patches = table.shape[0]
    source = lax.broadcasted_iota(jnp.int32, (LANES, 3 * LANES), 0)
    lane_of = lax.broadcasted_iota(jnp.int32, (LANES, 3 * LANES), 1)
    wanted = lane_of // LANES * NZ + lane_of % NZ
    spread = jnp.where(source == wanted, 1.0, 0.0).astype(jnp.float32)
    tables[...] = matmul(table, spread, ((1,), (0,)))

    for kind in range(2):
        base_sends[kind][0].wait_recv()

    @pl.when(has_across)
    def _():
        for kind in range(2):
            base_sends[kind][2].start()
        for kind in range(2):
            base_sends[kind][1].wait_recv()

    @pl.when(has_outward)
    def _():
        for kind in range(2):
            base_sends[kind][2].wait_recv()

    row_source = lax.broadcasted_iota(jnp.int32, (LANES, plane_cells), 0)
    row_lane = lax.broadcasted_iota(jnp.int32, (LANES, plane_cells), 1)
    row_spread = jnp.where(row_source == row_lane // NZ, 1.0, 0.0).astype(jnp.float32)

    def make_cells(place, carry):
        patch = matmul(near_ids[place], row_spread, ((1,), (0,)))
        zero = jnp.zeros(patch.shape, jnp.float32)

        def look(step, metric):
            rows = tables[pl.ds(pl.multiple_of(TILE * step, TILE), TILE), :]
            for row in range(TILE):
                here = patch == (TILE * step + row).astype(jnp.float32)
                metric = tuple(
                    jnp.where(
                        here,
                        jnp.concatenate(
                            [rows[row : row + 1, kind * LANES : (kind + 1) * LANES]] * tiles, axis=1
                        ),
                        value,
                    )
                    for kind, value in enumerate(metric)
                )
            return metric

        metric = lax.fori_loop(0, patches // TILE, look, (zero, zero, zero))
        kinetic = [value * (-1.0 / HALF_WIDTH) for value in metric]
        centre = (near_pot[place] - CENTRE) * (2.0 / HALF_WIDTH) + WEIGHTS[2] * (
            kinetic[0] + kinetic[1] + kinetic[2]
        )
        for kind, value in enumerate([centre] + [FIRST * value for value in kinetic]):
            for plane in range(planes):
                cells[place * planes + plane, kind : kind + 1] = value[plane : plane + 1]
        return carry

    lax.fori_loop(0, 4, make_cells, 0)
    for place, missing in missing_places:

        @pl.when(missing)
        def _():
            for plane in range(place * planes, (place + 1) * planes):
                cells[plane] = jnp.zeros(cells.shape[1:], jnp.float32)

    start_factor(pending, pending.shape[0])
    lane = lax.broadcasted_iota(jnp.int32, (TILE, LANES), 1)
    depth_at = lane % NZ
    zero_tile = jnp.zeros((TILE, LANES), jnp.float32)

    def mask(inside, weight):
        return jnp.where(inside, weight, 0.0).astype(jnp.float32)

    back_one, fore_one = mask(depth_at >= 1, 1.0), mask(depth_at < NZ - 1, 1.0)
    back_two, fore_two = mask(depth_at >= 2, RATIO), mask(depth_at < NZ - 2, RATIO)
    first_row, front_half, not_last = lane < NZ, lane < 2 * NZ, lane < 3 * NZ

    def roll(value, amount):
        return pltpu.roll(value, amount, axis=1)

    def apply(step, chunk):
        edge = REACH * (step + 1)

        def some_planes(number, carry):
            first = edge + GROUP * number
            results = []
            state = []
            for k in range(GROUP):
                value = grids[step, chunk, first + k, :, 0:LANES]
                state.append((value, zero_tile, roll(value, 2 * NZ), roll(value, 3 * NZ), zero_tile))
            for tile in range(tiles):
                columns = slice(tile * LANES, (tile + 1) * LANES)
                for k in range(GROUP):
                    here = first + k
                    value, two_before, two_here, one_after, one_before = state[k]
                    one_here = roll(value, NZ)
                    if tile < tiles - 1:
                        following = grids[step, chunk, here, :, (tile + 1) * LANES : (tile + 2) * LANES]
                        two_after, one_next = roll(following, 2 * NZ), roll(following, 3 * NZ)
                    else:
                        following, two_after, one_next = None, zero_tile, zero_tile
                    state[k] = (following, two_here, two_after, one_next, one_here)

                    def plane(shift):
                        return grids[step, chunk, here + shift, :, columns]

                    def cell(kind):
                        return cells[here, kind : kind + 1, columns]

                    total = cell(0) * value
                    total = total + cell(1) * (
                        (plane(-1) + plane(1)) - (plane(-2) + plane(2)) * RATIO
                    )
                    near = jnp.where(first_row, one_before, one_here) + jnp.where(
                        not_last, one_after, one_next
                    )
                    far = two_here + jnp.where(front_half, two_before, two_after)
                    total = total + cell(2) * (near - far * RATIO)
                    along = (back_one * roll(value, 1) + fore_one * roll(value, LANES - 1)) - (
                        back_two * roll(value, 2) + fore_two * roll(value, LANES - 2)
                    )
                    total = total + cell(3) * along
                    if step > 0:
                        total = total - grids[step - 1, chunk, here, :, columns]
                    else:
                        total = total * 0.5
                    results.append((here, columns, total))
            for here, columns, total in results:
                if step < DEGREE - 1:
                    grids[step + 1, chunk, here, :, columns] = total
                else:
                    last[chunk, here - planes, :, columns] = total
            return carry

        lax.fori_loop(0, (span - 2 * edge) // GROUP, some_planes, 0)

    def leave(chunk):
        rows = pl.ds(pl.multiple_of(band * held + side * half + chunk * TILE, TILE), TILE)
        for turn in range(bands):
            target = lax.rem(band + turn, bands)
            columns = pl.ds(pl.multiple_of(target * share, share), share)
            for other in (1, 0):
                source = last.at[chunk, slab(side if other == 0 else 1 - side), :, columns]
                landing = out.at[:, rows, :]
                if turn == 0 and other == 0:
                    pltpu.make_async_copy(source, landing, out_recv.at[0]).start()
                else:
                    pltpu.make_async_remote_copy(
                        src_ref=source,
                        dst_ref=landing,
                        send_sem=out_send.at[0],
                        recv_sem=out_recv.at[0],
                        device_id=to(target, space if other == 0 else partner),
                        device_id_type=MESH,
                    ).start()

    def finish(chunk):
        @pl.when(has_across)
        def _():
            halo_own[chunk].wait_recv()

        @pl.when(has_outward)
        def _():
            halo_passed[chunk].wait_recv()

        for step in range(DEGREE):
            apply(step, chunk)
        leave(chunk)

    for chunk in range(chunks):
        keep[chunk].wait()
        enter[chunk].wait_recv()

        @pl.when(has_across)
        def _():
            halo_passed[chunk].start()

        if chunk + 2 < chunks:
            begin(chunk + 2)
        if chunk > 0:
            finish(chunk - 1)
    finish(chunks - 1)

    for kind in range(2):
        base_sends[kind][0].wait_send()
    for chunk in range(chunks):
        enter[chunk].wait_send()

    @pl.when(has_outward)
    def _():
        for kind in range(2):
            base_sends[kind][1].wait_send()
        for chunk in range(chunks):
            halo_own[chunk].wait_send()

    @pl.when(has_across)
    def _():
        for kind in range(2):
            base_sends[kind][2].wait_send()
        for chunk in range(chunks):
            halo_passed[chunk].wait_send()

    pltpu.make_async_copy(out, out, out_recv.at[0]).wait()
    size = out.shape[1]
    middle = size // 2
    for plane in range(planes):
        high[plane], low[plane] = split(out[plane])

    def gram_of(first, last):
        begin = first // LANES * LANES
        sums = None
        for plane in range(planes):
            term = product(
                (high[plane, first:last], low[plane, first:last]),
                (high[plane, begin:], low[plane, begin:]),
                ((1,), (1,)),
            )
            sums = term if sums is None else sums + term
        return sums

    begin, relay, arrived, settle = start_reduction(
        bands, spaces, cell_total, local, near, far, mine, final, gram, gram_send, gram_recv
    )
    pieces = near.shape[0]
    depth = near.shape[2] * 2 * bands
    folded = pieces * depth < size
    first_rows = gram_of(0, 2 * depth if folded else depth)
    local[:depth] = first_rows[:depth]
    begin(0)
    if folded:
        in_front = lax.broadcasted_iota(jnp.int32, (depth, LANES), 1) < depth
        second = first_rows[depth:]
        both = gram_of(2 * depth, 4 * depth)
        local[depth : 2 * depth, :LANES] = jnp.where(
            in_front, pltpu.roll(both[depth:], depth, axis=1), second[:, :LANES]
        )
        local[depth : 2 * depth, LANES:] = second[:, LANES:]
        local[2 * depth : 3 * depth, middle:] = both[:depth]
    else:
        for piece in range(1, pieces):
            local[piece * depth : (piece + 1) * depth, piece * depth // LANES * LANES :] = gram_of(
                piece * depth, (piece + 1) * depth
            )
    for piece in range(1, pieces):
        begin(piece)
    relay()
    stores = []
    for first in range(0, size, BLOCK):
        piece = first // depth
        if first % depth == 0 and piece < pieces:
            arrived(piece)
        if piece < pieces:
            rows = gram[first : first + BLOCK, first // LANES * LANES :]
        else:
            rows = pltpu.roll(gram[depth : 2 * depth, :LANES], depth, axis=1)
        if first == middle:
            top = split(inverse[:middle, :middle])
            for plane in range(planes):
                result[plane, :middle] = product(
                    top, (high[plane, :middle], low[plane, :middle]), ((1,), (0,))
                )
        factor_rows(rows, pending, inverse, first, size)
    bottom = split(inverse[middle:, :])
    for plane in range(planes):
        result[plane, middle:] = product(bottom, (high[plane], low[plane]), ((1,), (0,)))
    settle()
    for copy in stores:
        copy.wait()
    sent = out.at[:, 0 : out.shape[1] - out.shape[1] // (2 * bands), :]
    pltpu.make_async_copy(sent, sent, out_send.at[0]).wait()


def on_device(states, patch_ids, metric_table, potential):
    held, planes, plane_cells = states.shape
    bands = lax.axis_size("band")
    spaces = lax.axis_size("space")
    chunks = held // 2 // TILE
    total = held * bands
    depth = max(BLOCK, 2 * bands * TILE)
    folded = depth == BLOCK and total == 4 * BLOCK and LANES == 2 * BLOCK
    pieces = total // depth - int(folded)
    share = depth // (2 * bands)
    if planes != REACH * DEGREE:
        raise ValueError("slab depth")
    dma = pltpu.SemaphoreType.DMA
    hbm = pl.BlockSpec(memory_space=pltpu.HBM)
    regrouped = (planes, total, plane_cells // bands)
    packed = jnp.concatenate(
        [
            jnp.pad(values, ((0, -values.shape[0] % TILE), (0, plane_cells - values.shape[1]))).astype(jnp.float32)
            for values in (potential, patch_ids, metric_table)
        ],
        axis=0,
    )
    result = pl.pallas_call(
        functools.partial(filter_kernel, bands, spaces, float(planes * plane_cells * spaces)),
        out_shape=jax.ShapeDtypeStruct(regrouped, jnp.float32),
        in_specs=[hbm, pl.BlockSpec(memory_space=pltpu.VMEM)],
        out_specs=pl.BlockSpec(memory_space=pltpu.VMEM),
        scratch_shapes=[
            pltpu.VMEM(regrouped, jnp.float32),
            pltpu.VMEM(regrouped, jnp.bfloat16),
            pltpu.VMEM(regrouped, jnp.bfloat16),
            pltpu.VMEM(regrouped, jnp.float32),
            pltpu.VMEM((total, total), jnp.float32),
            pltpu.VMEM((pieces, 2 * bands - 1, share, total), jnp.float32),
            pltpu.VMEM((pieces, spaces // 2, share, total), jnp.float32),
            pltpu.VMEM((pieces, share, total), jnp.float32),
            pltpu.VMEM((pieces, share, total), jnp.float32),
            pltpu.VMEM((total, total), jnp.float32),
            pltpu.VMEM((total, 2 * total), jnp.float32),
            pltpu.VMEM((total, total), jnp.float32),
            pltpu.VMEM((DEGREE, chunks, 4 * planes, TILE, plane_cells), jnp.float32),
            pltpu.VMEM((chunks, 2 * planes, TILE, plane_cells), jnp.float32),
            pltpu.VMEM((4 * planes, 4, plane_cells), jnp.float32),
            pltpu.VMEM((4, TILE, LANES), jnp.float32),
            pltpu.VMEM((4, TILE, plane_cells), jnp.float32),
            pltpu.VMEM((metric_table.shape[0], 3 * LANES), jnp.float32),
            dma((2, 3)),
            dma((2, 3)),
            dma((chunks,)),
            dma((chunks,)),
            dma((chunks,)),
            dma((2, chunks)),
            dma((2, chunks)),
            dma((1,)),
            dma((1,)),
            dma((2, planes)),
            dma((3, pieces)),
            dma((3, pieces)),
        ],
        compiler_params=pltpu.CompilerParams(
            collective_id=0, has_side_effects=True, vmem_limit_bytes=52 * 2**20
        ),
        name="orthonormal_states",
    )(states.transpose(1, 0, 2), packed)
    return result.transpose(1, 0, 2)


def solution(mesh):
    return jax.shard_map(
        on_device,
        mesh=mesh,
        in_specs=(P("band", "space", None), P("space", None), P(), P("space", None)),
        out_specs=P(None, "space", "band"),
        check_vma=False,
    )
```

```python
import functools

import jax
import jax.numpy as jnp
from jax import lax
from jax.experimental import pallas as pl
from jax.experimental.pallas import tpu as pltpu
from jax.sharding import PartitionSpec as P

DEGREE = 3
NZ = 32


CENTRE = 8.5
HALF_WIDTH = 7.5
WEIGHTS = (-1.0 / 12.0, 4.0 / 3.0, -2.5, 4.0 / 3.0, -1.0 / 12.0)


MESH = pl.DeviceIdType.MESH
HIGHEST = lax.Precision.HIGHEST
BLOCK = 64
TILE = 8
STRIP = 16
LANES = 128


def matmul(left, right, dims):
    return lax.dot_general(
        left, right, (dims, ((), ())), precision=HIGHEST, preferred_element_type=jnp.float32
    )


def factor_block(diagonal):
    size = diagonal.shape[0]
    rows = lax.broadcasted_iota(jnp.int32, (size, size), 0)
    columns = lax.broadcasted_iota(jnp.int32, (size, size), 1)
    unit = jnp.where(rows == columns, 1.0, 0.0).astype(jnp.float32)
    rest = jnp.concatenate([diagonal, unit], axis=1)
    width = rest.shape[1]
    in_strip = lax.broadcasted_iota(jnp.int32, (STRIP, width), 0)
    done = []
    for start in range(0, size, STRIP):
        top, rest = rest[:STRIP], rest[STRIP:]
        panel = [
            jnp.broadcast_to(top[:, start + k : start + k + 1], top.shape) for k in range(STRIP)
        ]
        scale = jnp.zeros((STRIP, width), jnp.float32)
        for group in range(0, STRIP, TILE):
            weights, eliminated = {}, []
            for k in range(group, group + TILE):
                inverse = 1.0 / panel[k][k : k + 1, :]
                scale = jnp.where(in_strip == k, inverse, scale)
                below = jnp.where(in_strip > k, panel[k], 0.0)
                row = top[k : k + 1, :] * inverse
                for later in range(k + 1, STRIP):
                    weights[k, later] = panel[later][k : k + 1, :] * inverse
                    panel[later] = panel[later] - below * weights[k, later]
                top = top - below * row
                eliminated.append(row)
            if size - start > STRIP:
                columns_of = [
                    jnp.broadcast_to(rest[:, start + k : start + k + 1], rest.shape)
                    for k in range(group, group + TILE)
                ]
                total = None
                for k in range(TILE):
                    for later in range(k + 1, TILE):
                        columns_of[later] = (
                            columns_of[later] - columns_of[k] * weights[group + k, group + later]
                        )
                    term = columns_of[k] * eliminated[k]
                    total = term if total is None else total + term
                rest = rest - total
        done.append(top * jnp.sqrt(scale))
    return jnp.concatenate(done, axis=0)[:, size:]


def start_factor(pending, size):
    rows = lax.broadcasted_iota(jnp.int32, (size, 2 * size), 0)
    columns = lax.broadcasted_iota(jnp.int32, (size, 2 * size), 1)
    pending[...] = jnp.where(columns == rows + size, 1.0, 0.0).astype(jnp.float32)


def factor_rows(gram_rows, pending, inverse, first, size):
    last = first + BLOCK
    low = first // LANES * LANES
    high = size + -(-last // LANES) * LANES
    current = jnp.concatenate(
        [
            gram_rows + pending[first:last, low:size],
            pending[first:last, size:high],
        ],
        axis=1,
    )
    small = factor_block(current[:, first - low : last - low])
    rows = matmul(small, current, ((1,), (0,)))
    inverse[first:last, 0 : high - size] = rows[:, size - low :]
    if last < size:
        aligned = last // LANES * LANES
        update = matmul(rows[:, aligned - low : size - low], rows, ((0,), (0,)))
        pending[last:, low:high] -= update[last - aligned :]


def start_reduction(bands, spaces, cell_total, local, near, far, mine, final, gram, send_sems, recv_sems):
    size = local.shape[0]
    near_count, far_count = 2 * bands, spaces // 2
    pieces, share = near.shape[0], near.shape[2]
    depth = share * near_count
    band, space = lax.axis_index("band"), lax.axis_index("space")
    line = space // 2
    side = space - 2 * line
    place = 2 * band + side

    def rows_of(piece, index):
        return pl.ds(pl.multiple_of(piece * depth + index * share, share), share)

    def columns_of(piece):
        return slice(piece * depth // LANES * LANES, size)

    def near_peer(offset):
        index = lax.rem(place + offset, near_count)
        return index, {"band": index // 2, "space": 2 * line + lax.rem(index, 2)}

    def far_peer(offset):
        return {"band": band, "space": 2 * lax.rem(line + offset, far_count) + side}

    def send(source, landing, stage, piece, target):
        pltpu.make_async_remote_copy(
            src_ref=source,
            dst_ref=landing,
            send_sem=send_sems.at[stage, piece],
            recv_sem=recv_sems.at[stage, piece],
            device_id=target,
            device_id_type=MESH,
        ).start()

    def bytes_of(stage, piece):
        columns = columns_of(piece)
        if stage == 1:
            return far.at[piece, 0 : far_count - 1, :, columns]
        return near.at[piece, :, :, columns]

    def wait(sems, stage, piece):
        moved = bytes_of(stage, piece)
        pltpu.make_async_copy(moved, moved, sems.at[stage, piece]).wait()

    def begin(piece):
        columns = columns_of(piece)
        for offset in range(1, near_count):
            index, target = near_peer(offset)
            send(
                local.at[rows_of(piece, index), columns], near.at[piece, offset - 1, :, columns],
                0, piece, target,
            )

    def relay():
        for piece in range(pieces):
            columns = columns_of(piece)
            wait(recv_sems, 0, piece)
            mine[piece, :, columns] = (
                jnp.sum(near[piece, :, :, columns], axis=0) + local[rows_of(piece, place), columns]
            )
            for offset in range(1, far_count):
                send(
                    mine.at[piece, :, columns], far.at[piece, line, :, columns], 1, piece,
                    far_peer(offset),
                )
        for piece in range(pieces):
            columns = columns_of(piece)
            wait(recv_sems, 1, piece)
            far[piece, line, :, columns] = mine[piece, :, columns]
            final[piece, :, columns] = jnp.sum(far[piece, :, :, columns], axis=0) / cell_total
            for offset in range(1, near_count):
                send(
                    final.at[piece, :, columns], gram.at[rows_of(piece, place), columns], 2, piece,
                    near_peer(offset)[1],
                )

    def arrived(piece):
        columns = columns_of(piece)
        wait(recv_sems, 2, piece)
        gram[rows_of(piece, place), columns] = final[piece, :, columns]

    def settle():
        for stage in range(3):
            for piece in range(pieces):
                wait(send_sems, stage, piece)

    return begin, relay, arrived, settle


FIRST = 4.0 / 3.0
RATIO = 1.0 / 16.0
REACH = 2
GROUP = 4


def split(value):
    high = value.astype(jnp.bfloat16)
    return high, (value - high.astype(jnp.float32)).astype(jnp.bfloat16)


def product(left, right, dims):
    left_high, left_low = left
    right_high, right_low = right

    def one(first, second):
        return lax.dot_general(first, second, (dims, ((), ())), preferred_element_type=jnp.float32)

    return one(left_high, right_high) + (one(left_high, right_low) + one(left_low, right_high))


def filter_kernel(
    bands, spaces, cell_total, states, packed, result, out, high, low, staged,
    local, near, far, mine, final, gram, pending, inverse, grids, last, cells, near_ids, near_pot,
    tables, base_send, base_recv, in_send, in_recv, keep_sems, halo_send, halo_recv, out_send,
    out_recv, store_sems, gram_send, gram_recv,
):
    planes, held, plane_cells = states.shape
    half = held // 2
    chunks = half // TILE
    span = 4 * planes
    share = plane_cells // bands
    tiles = plane_cells // LANES
    band = lax.axis_index("band")
    space = lax.axis_index("space")
    side = lax.rem(space, 2)
    partner = space + 1 - 2 * side
    outward = space + 4 * side - 2
    across = space - 4 * side + 2
    has_outward = jnp.logical_and(outward >= 0, outward < spaces)
    has_across = jnp.logical_and(across >= 0, across < spaces)

    def to(target_band, target_space):
        return {"band": target_band, "space": target_space}

    own, theirs = 1 + side, 2 - side
    potential = packed.at[0:TILE]
    ids = packed.at[TILE : 2 * TILE, 0:LANES]
    table = packed[2 * TILE :, 0:LANES]

    barrier = pltpu.get_barrier_semaphore()
    for turn in range(bands):
        target = lax.rem(band + turn, bands)
        if turn:
            pl.semaphore_signal(
                barrier, inc=1, device_id=to(target, space), device_id_type=MESH
            )
        pl.semaphore_signal(barrier, inc=1, device_id=to(target, partner), device_id_type=MESH)
    lines = spaces // 2
    for offset in range(1, lines):
        pl.semaphore_signal(
            barrier,
            inc=1,
            device_id=to(band, 2 * lax.rem(space // 2 + offset, lines) + side),
            device_id_type=MESH,
        )
    pl.semaphore_wait(barrier, 2 * bands + lines - 2)

    def slab(place):
        return pl.ds(place * planes, planes)

    def rows_of(part, chunk):
        return pl.ds(pl.multiple_of(part * half + chunk * TILE, TILE), TILE)

    def remote(source, landing, send_sem, recv_sem, target):
        return pltpu.make_async_remote_copy(
            src_ref=source,
            dst_ref=landing,
            send_sem=send_sem,
            recv_sem=recv_sem,
            device_id=to(band, target),
            device_id_type=MESH,
        )

    own_landing, passed_landing = 3 * (1 - side), 3 * side
    base_sends = []
    for kind, (source, landing) in enumerate(((ids, near_ids), (potential, near_pot))):
        base_sends.append(
            (
                remote(source, landing.at[own], base_send.at[kind, 0], base_recv.at[kind, 0], partner),
                remote(source, landing.at[own_landing], base_send.at[kind, 1], base_recv.at[kind, 1], outward),
                remote(
                    landing.at[theirs], landing.at[passed_landing],
                    base_send.at[kind, 2], base_recv.at[kind, 2], across,
                ),
            )
        )
    enter, keep, halo_own, halo_passed = [], [], [], []
    for chunk in range(chunks):
        grid = grids.at[0, chunk]
        kept = states.at[:, rows_of(side, chunk)]
        enter.append(
            remote(
                states.at[:, rows_of(1 - side, chunk)], grid.at[slab(own)],
                in_send.at[chunk], in_recv.at[chunk], partner,
            )
        )
        keep.append(pltpu.make_async_copy(kept, grid.at[slab(own)], keep_sems.at[chunk]))
        halo_own.append(
            remote(
                kept, grid.at[slab(own_landing)],
                halo_send.at[0, chunk], halo_recv.at[0, chunk], outward,
            )
        )
        halo_passed.append(
            remote(
                grid.at[slab(theirs)], grid.at[slab(passed_landing)],
                halo_send.at[1, chunk], halo_recv.at[1, chunk], across,
            )
        )

    def begin(chunk):
        enter[chunk].start()

        @pl.when(has_outward)
        def _():
            halo_own[chunk].start()

    for kind in range(2):
        base_sends[kind][0].start()

    @pl.when(has_outward)
    def _():
        for kind in range(2):
            base_sends[kind][1].start()

    for chunk in range(min(2, chunks)):
        begin(chunk)
    for chunk in range(chunks):
        keep[chunk].start()
    near_ids[own] = ids[...]
    near_pot[own] = potential[...]
    missing_places = ((0, space < 2), (3, space >= spaces - 2))
    for place, missing in missing_places:

        @pl.when(missing)
        def _():
            near_ids[place] = jnp.zeros(near_ids.shape[1:], jnp.float32)
            near_pot[place] = jnp.zeros(near_pot.shape[1:], jnp.float32)
            for chunk in range(chunks):
                for plane in range(place * planes, (place + 1) * planes):
                    grids[0, chunk, plane] = jnp.zeros((TILE, plane_cells), jnp.float32)

    patches = table.shape[0]
    source = lax.broadcasted_iota(jnp.int32, (LANES, 3 * LANES), 0)
    lane_of = lax.broadcasted_iota(jnp.int32, (LANES, 3 * LANES), 1)
    wanted = lane_of // LANES * NZ + lane_of % NZ
    spread = jnp.where(source == wanted, 1.0, 0.0).astype(jnp.float32)
    tables[...] = matmul(table, spread, ((1,), (0,)))

    for kind in range(2):
        base_sends[kind][0].wait_recv()

    @pl.when(has_across)
    def _():
        for kind in range(2):
            base_sends[kind][2].start()
        for kind in range(2):
            base_sends[kind][1].wait_recv()

    @pl.when(has_outward)
    def _():
        for kind in range(2):
            base_sends[kind][2].wait_recv()

    row_source = lax.broadcasted_iota(jnp.int32, (LANES, plane_cells), 0)
    row_lane = lax.broadcasted_iota(jnp.int32, (LANES, plane_cells), 1)
    row_spread = jnp.where(row_source == row_lane // NZ, 1.0, 0.0).astype(jnp.float32)

    def make_cells(place, carry):
        patch = matmul(near_ids[place], row_spread, ((1,), (0,)))
        zero = jnp.zeros(patch.shape, jnp.float32)

        def look(step, metric):
            rows = tables[pl.ds(pl.multiple_of(TILE * step, TILE), TILE), :]
            for row in range(TILE):
                here = patch == (TILE * step + row).astype(jnp.float32)
                metric = tuple(
                    jnp.where(
                        here,
                        jnp.concatenate(
                            [rows[row : row + 1, kind * LANES : (kind + 1) * LANES]] * tiles, axis=1
                        ),
                        value,
                    )
                    for kind, value in enumerate(metric)
                )
            return metric

        metric = lax.fori_loop(0, patches // TILE, look, (zero, zero, zero))
        kinetic = [value * (-1.0 / HALF_WIDTH) for value in metric]
        centre = (near_pot[place] - CENTRE) * (2.0 / HALF_WIDTH) + WEIGHTS[2] * (
            kinetic[0] + kinetic[1] + kinetic[2]
        )
        for kind, value in enumerate([centre] + [FIRST * value for value in kinetic]):
            for plane in range(planes):
                cells[place * planes + plane, kind : kind + 1] = value[plane : plane + 1]
        return carry

    lax.fori_loop(0, 4, make_cells, 0)
    for place, missing in missing_places:

        @pl.when(missing)
        def _():
            for plane in range(place * planes, (place + 1) * planes):
                cells[plane] = jnp.zeros(cells.shape[1:], jnp.float32)

    start_factor(pending, pending.shape[0])
    lane = lax.broadcasted_iota(jnp.int32, (TILE, LANES), 1)
    depth_at = lane % NZ
    zero_tile = jnp.zeros((TILE, LANES), jnp.float32)

    def mask(inside, weight):
        return jnp.where(inside, weight, 0.0).astype(jnp.float32)

    back_one, fore_one = mask(depth_at >= 1, 1.0), mask(depth_at < NZ - 1, 1.0)
    back_two, fore_two = mask(depth_at >= 2, RATIO), mask(depth_at < NZ - 2, RATIO)
    first_row, front_half, not_last = lane < NZ, lane < 2 * NZ, lane < 3 * NZ

    def roll(value, amount):
        return pltpu.roll(value, amount, axis=1)

    def apply(step, chunk):
        edge = REACH * (step + 1)

        def some_planes(number, carry):
            first = edge + GROUP * number
            results = []
            state = []
            for k in range(GROUP):
                value = grids[step, chunk, first + k, :, 0:LANES]
                state.append((value, zero_tile, roll(value, 2 * NZ), roll(value, 3 * NZ), zero_tile))
            for tile in range(tiles):
                columns = slice(tile * LANES, (tile + 1) * LANES)
                for k in range(GROUP):
                    here = first + k
                    value, two_before, two_here, one_after, one_before = state[k]
                    one_here = roll(value, NZ)
                    if tile < tiles - 1:
                        following = grids[step, chunk, here, :, (tile + 1) * LANES : (tile + 2) * LANES]
                        two_after, one_next = roll(following, 2 * NZ), roll(following, 3 * NZ)
                    else:
                        following, two_after, one_next = None, zero_tile, zero_tile
                    state[k] = (following, two_here, two_after, one_next, one_here)

                    def plane(shift):
                        return grids[step, chunk, here + shift, :, columns]

                    def cell(kind):
                        return cells[here, kind : kind + 1, columns]

                    total = cell(0) * value
                    total = total + cell(1) * (
                        (plane(-1) + plane(1)) - (plane(-2) + plane(2)) * RATIO
                    )
                    near = jnp.where(first_row, one_before, one_here) + jnp.where(
                        not_last, one_after, one_next
                    )
                    far = two_here + jnp.where(front_half, two_before, two_after)
                    total = total + cell(2) * (near - far * RATIO)
                    along = (back_one * roll(value, 1) + fore_one * roll(value, LANES - 1)) - (
                        back_two * roll(value, 2) + fore_two * roll(value, LANES - 2)
                    )
                    total = total + cell(3) * along
                    if step > 0:
                        total = total - grids[step - 1, chunk, here, :, columns]
                    else:
                        total = total * 0.5
                    results.append((here, columns, total))
            for here, columns, total in results:
                if step < DEGREE - 1:
                    grids[step + 1, chunk, here, :, columns] = total
                else:
                    last[chunk, here - planes, :, columns] = total
            return carry

        lax.fori_loop(0, (span - 2 * edge) // GROUP, some_planes, 0)

    def leave(chunk):
        rows = pl.ds(pl.multiple_of(band * held + side * half + chunk * TILE, TILE), TILE)
        for turn in range(bands):
            target = lax.rem(band + turn, bands)
            columns = pl.ds(pl.multiple_of(target * share, share), share)
            for other in (1, 0):
                source = last.at[chunk, slab(side if other == 0 else 1 - side), :, columns]
                landing = out.at[:, rows, :]
                if turn == 0 and other == 0:
                    pltpu.make_async_copy(source, landing, out_recv.at[0]).start()
                else:
                    pltpu.make_async_remote_copy(
                        src_ref=source,
                        dst_ref=landing,
                        send_sem=out_send.at[0],
                        recv_sem=out_recv.at[0],
                        device_id=to(target, space if other == 0 else partner),
                        device_id_type=MESH,
                    ).start()

    def finish(chunk):
        @pl.when(has_across)
        def _():
            halo_own[chunk].wait_recv()

        @pl.when(has_outward)
        def _():
            halo_passed[chunk].wait_recv()

        for step in range(DEGREE):
            apply(step, chunk)
        leave(chunk)

    for chunk in range(chunks):
        keep[chunk].wait()
        enter[chunk].wait_recv()

        @pl.when(has_across)
        def _():
            halo_passed[chunk].start()

        if chunk + 2 < chunks:
            begin(chunk + 2)
        if chunk > 0:
            finish(chunk - 1)
    finish(chunks - 1)

    for kind in range(2):
        base_sends[kind][0].wait_send()
    for chunk in range(chunks):
        enter[chunk].wait_send()

    @pl.when(has_outward)
    def _():
        for kind in range(2):
            base_sends[kind][1].wait_send()
        for chunk in range(chunks):
            halo_own[chunk].wait_send()

    @pl.when(has_across)
    def _():
        for kind in range(2):
            base_sends[kind][2].wait_send()
        for chunk in range(chunks):
            halo_passed[chunk].wait_send()

    pltpu.make_async_copy(out, out, out_recv.at[0]).wait()
    size = out.shape[1]
    middle = size // 2
    for plane in range(planes):
        high[plane], low[plane] = split(out[plane])

    def gram_of(first, last):
        begin = first // LANES * LANES
        sums = None
        for plane in range(planes):
            term = product(
                (high[plane, first:last], low[plane, first:last]),
                (high[plane, begin:], low[plane, begin:]),
                ((1,), (1,)),
            )
            sums = term if sums is None else sums + term
        return sums

    begin, relay, arrived, settle = start_reduction(
        bands, spaces, cell_total, local, near, far, mine, final, gram, gram_send, gram_recv
    )
    pieces = near.shape[0]
    depth = near.shape[2] * 2 * bands
    folded = pieces * depth < size
    first_rows = gram_of(0, 2 * depth if folded else depth)
    local[:depth] = first_rows[:depth]
    begin(0)
    if folded:
        in_front = lax.broadcasted_iota(jnp.int32, (depth, LANES), 1) < depth
        second = first_rows[depth:]
        both = gram_of(2 * depth, 4 * depth)
        local[depth : 2 * depth, :LANES] = jnp.where(
            in_front, pltpu.roll(both[depth:], depth, axis=1), second[:, :LANES]
        )
        local[depth : 2 * depth, LANES:] = second[:, LANES:]
        local[2 * depth : 3 * depth, middle:] = both[:depth]
    else:
        for piece in range(1, pieces):
            local[piece * depth : (piece + 1) * depth, piece * depth // LANES * LANES :] = gram_of(
                piece * depth, (piece + 1) * depth
            )
    for piece in range(1, pieces):
        begin(piece)
    relay()
    stores = []
    for first in range(0, size, BLOCK):
        piece = first // depth
        if first % depth == 0 and piece < pieces:
            arrived(piece)
        if piece < pieces:
            rows = gram[first : first + BLOCK, first // LANES * LANES :]
        else:
            rows = pltpu.roll(gram[depth : 2 * depth, :LANES], depth, axis=1)
        if first == middle:
            top = split(inverse[:middle, :middle])
            for plane in range(planes):
                result[plane, :middle] = product(
                    top, (high[plane, :middle], low[plane, :middle]), ((1,), (0,))
                )
        factor_rows(rows, pending, inverse, first, size)
    bottom = split(inverse[middle:, :])
    for plane in range(planes):
        result[plane, middle:] = product(bottom, (high[plane], low[plane]), ((1,), (0,)))
    settle()
    for copy in stores:
        copy.wait()
    sent = out.at[:, 0 : out.shape[1] - out.shape[1] // (2 * bands), :]
    pltpu.make_async_copy(sent, sent, out_send.at[0]).wait()


def on_device(states, patch_ids, metric_table, potential):
    held, planes, plane_cells = states.shape
    bands = lax.axis_size("band")
    spaces = lax.axis_size("space")
    chunks = held // 2 // TILE
    total = held * bands
    depth = max(BLOCK, 2 * bands * TILE)
    folded = depth == BLOCK and total == 4 * BLOCK and LANES == 2 * BLOCK
    pieces = total // depth - int(folded)
    share = depth // (2 * bands)
    if planes != REACH * DEGREE:
        raise ValueError("slab depth")
    dma = pltpu.SemaphoreType.DMA
    hbm = pl.BlockSpec(memory_space=pltpu.HBM)
    regrouped = (planes, total, plane_cells // bands)
    height = 2 * TILE + metric_table.shape[0]
    packed = None
    for first, values in ((0, potential), (TILE, patch_ids), (2 * TILE, metric_table)):
        rows, columns = values.shape
        placed = jnp.pad(
            values, ((first, height - first - rows), (0, plane_cells - columns))
        ).astype(jnp.float32)
        packed = placed if packed is None else packed + placed
    result = pl.pallas_call(
        functools.partial(filter_kernel, bands, spaces, float(planes * plane_cells * spaces)),
        out_shape=jax.ShapeDtypeStruct(regrouped, jnp.float32),
        in_specs=[hbm, pl.BlockSpec(memory_space=pltpu.VMEM)],
        out_specs=pl.BlockSpec(memory_space=pltpu.VMEM),
        scratch_shapes=[
            pltpu.VMEM(regrouped, jnp.float32),
            pltpu.VMEM(regrouped, jnp.bfloat16),
            pltpu.VMEM(regrouped, jnp.bfloat16),
            pltpu.VMEM(regrouped, jnp.float32),
            pltpu.VMEM((total, total), jnp.float32),
            pltpu.VMEM((pieces, 2 * bands - 1, share, total), jnp.float32),
            pltpu.VMEM((pieces, spaces // 2, share, total), jnp.float32),
            pltpu.VMEM((pieces, share, total), jnp.float32),
            pltpu.VMEM((pieces, share, total), jnp.float32),
            pltpu.VMEM((total, total), jnp.float32),
            pltpu.VMEM((total, 2 * total), jnp.float32),
            pltpu.VMEM((total, total), jnp.float32),
            pltpu.VMEM((DEGREE, chunks, 4 * planes, TILE, plane_cells), jnp.float32),
            pltpu.VMEM((chunks, 2 * planes, TILE, plane_cells), jnp.float32),
            pltpu.VMEM((4 * planes, 4, plane_cells), jnp.float32),
            pltpu.VMEM((4, TILE, LANES), jnp.float32),
            pltpu.VMEM((4, TILE, plane_cells), jnp.float32),
            pltpu.VMEM((metric_table.shape[0], 3 * LANES), jnp.float32),
            dma((2, 3)),
            dma((2, 3)),
            dma((chunks,)),
            dma((chunks,)),
            dma((chunks,)),
            dma((2, chunks)),
            dma((2, chunks)),
            dma((1,)),
            dma((1,)),
            dma((2, planes)),
            dma((3, pieces)),
            dma((3, pieces)),
        ],
        compiler_params=pltpu.CompilerParams(
            collective_id=0, has_side_effects=True, vmem_limit_bytes=52 * 2**20
        ),
        name="orthonormal_states",
    )(states.transpose(1, 0, 2), packed)
    return result.transpose(1, 0, 2)


def solution(mesh):
    return jax.shard_map(
        on_device,
        mesh=mesh,
        in_specs=(P("band", "space", None), P("space", None), P(), P("space", None)),
        out_specs=P(None, "space", "band"),
        check_vma=False,
    )
```

```python
import functools

import jax
import jax.numpy as jnp
from jax import lax
from jax.experimental import pallas as pl
from jax.experimental.pallas import tpu as pltpu
from jax.sharding import PartitionSpec as P

DEGREE = 3
NZ = 32


CENTRE = 8.5
HALF_WIDTH = 7.5
WEIGHTS = (-1.0 / 12.0, 4.0 / 3.0, -2.5, 4.0 / 3.0, -1.0 / 12.0)


MESH = pl.DeviceIdType.MESH
HIGHEST = lax.Precision.HIGHEST
BLOCK = 64
TILE = 8
STRIP = 16
LANES = 128


def matmul(left, right, dims):
    return lax.dot_general(
        left, right, (dims, ((), ())), precision=HIGHEST, preferred_element_type=jnp.float32
    )


def factor_block(diagonal):
    size = diagonal.shape[0]
    rows = lax.broadcasted_iota(jnp.int32, (size, size), 0)
    columns = lax.broadcasted_iota(jnp.int32, (size, size), 1)
    unit = jnp.where(rows == columns, 1.0, 0.0).astype(jnp.float32)
    rest = jnp.concatenate([diagonal, unit], axis=1)
    width = rest.shape[1]
    in_strip = lax.broadcasted_iota(jnp.int32, (STRIP, width), 0)
    done = []
    for start in range(0, size, STRIP):
        top, rest = rest[:STRIP], rest[STRIP:]
        panel = [
            jnp.broadcast_to(top[:, start + k : start + k + 1], top.shape) for k in range(STRIP)
        ]
        scale = jnp.zeros((STRIP, width), jnp.float32)
        for group in range(0, STRIP, TILE):
            weights, eliminated = {}, []
            for k in range(group, group + TILE):
                inverse = 1.0 / panel[k][k : k + 1, :]
                scale = jnp.where(in_strip == k, inverse, scale)
                below = jnp.where(in_strip > k, panel[k], 0.0)
                row = top[k : k + 1, :] * inverse
                for later in range(k + 1, STRIP):
                    weights[k, later] = panel[later][k : k + 1, :] * inverse
                    panel[later] = panel[later] - below * weights[k, later]
                top = top - below * row
                eliminated.append(row)
            if size - start > STRIP:
                columns_of = [
                    jnp.broadcast_to(rest[:, start + k : start + k + 1], rest.shape)
                    for k in range(group, group + TILE)
                ]
                total = None
                for k in range(TILE):
                    for later in range(k + 1, TILE):
                        columns_of[later] = (
                            columns_of[later] - columns_of[k] * weights[group + k, group + later]
                        )
                    term = columns_of[k] * eliminated[k]
                    total = term if total is None else total + term
                rest = rest - total
        done.append(top * jnp.sqrt(scale))
    return jnp.concatenate(done, axis=0)[:, size:]


def start_factor(pending, size):
    rows = lax.broadcasted_iota(jnp.int32, (size, 2 * size), 0)
    columns = lax.broadcasted_iota(jnp.int32, (size, 2 * size), 1)
    pending[...] = jnp.where(columns == rows + size, 1.0, 0.0).astype(jnp.float32)


def factor_rows(gram_rows, pending, inverse, first, size):
    last = first + BLOCK
    low = first // LANES * LANES
    high = size + -(-last // LANES) * LANES
    current = jnp.concatenate(
        [
            gram_rows + pending[first:last, low:size],
            pending[first:last, size:high],
        ],
        axis=1,
    )
    small = factor_block(current[:, first - low : last - low])
    rows = matmul(small, current, ((1,), (0,)))
    inverse[first:last, 0 : high - size] = rows[:, size - low :]
    if last < size:
        aligned = last // LANES * LANES
        update = matmul(rows[:, aligned - low : size - low], rows, ((0,), (0,)))
        pending[last:, low:high] -= update[last - aligned :]


def start_reduction(bands, spaces, cell_total, local, near, far, mine, final, gram, send_sems, recv_sems):
    size = local.shape[0]
    near_count, far_count = 2 * bands, spaces // 2
    pieces, share = near.shape[0], near.shape[2]
    depth = share * near_count
    band, space = lax.axis_index("band"), lax.axis_index("space")
    line = space // 2
    side = space - 2 * line
    place = 2 * band + side

    def rows_of(piece, index):
        return pl.ds(pl.multiple_of(piece * depth + index * share, share), share)

    def columns_of(piece):
        return slice(piece * depth // LANES * LANES, size)

    def near_peer(offset):
        index = lax.rem(place + offset, near_count)
        return index, {"band": index // 2, "space": 2 * line + lax.rem(index, 2)}

    def far_peer(offset):
        return {"band": band, "space": 2 * lax.rem(line + offset, far_count) + side}

    def send(source, landing, stage, piece, target):
        pltpu.make_async_remote_copy(
            src_ref=source,
            dst_ref=landing,
            send_sem=send_sems.at[stage, piece],
            recv_sem=recv_sems.at[stage, piece],
            device_id=target,
            device_id_type=MESH,
        ).start()

    def bytes_of(stage, piece):
        columns = columns_of(piece)
        if stage == 1:
            return far.at[piece, 0 : far_count - 1, :, columns]
        return near.at[piece, :, :, columns]

    def wait(sems, stage, piece):
        moved = bytes_of(stage, piece)
        pltpu.make_async_copy(moved, moved, sems.at[stage, piece]).wait()

    def begin(piece):
        columns = columns_of(piece)
        for offset in range(1, near_count):
            index, target = near_peer(offset)
            send(
                local.at[rows_of(piece, index), columns], near.at[piece, offset - 1, :, columns],
                0, piece, target,
            )

    def relay():
        for piece in range(pieces):
            columns = columns_of(piece)
            wait(recv_sems, 0, piece)
            mine[piece, :, columns] = (
                jnp.sum(near[piece, :, :, columns], axis=0) + local[rows_of(piece, place), columns]
            )
            for offset in range(1, far_count):
                send(
                    mine.at[piece, :, columns], far.at[piece, line, :, columns], 1, piece,
                    far_peer(offset),
                )
        for piece in range(pieces):
            columns = columns_of(piece)
            wait(recv_sems, 1, piece)
            far[piece, line, :, columns] = mine[piece, :, columns]
            final[piece, :, columns] = jnp.sum(far[piece, :, :, columns], axis=0) / cell_total
            for offset in range(1, near_count):
                send(
                    final.at[piece, :, columns], gram.at[rows_of(piece, place), columns], 2, piece,
                    near_peer(offset)[1],
                )

    def arrived(piece):
        columns = columns_of(piece)
        wait(recv_sems, 2, piece)
        gram[rows_of(piece, place), columns] = final[piece, :, columns]

    def settle():
        for stage in range(3):
            for piece in range(pieces):
                wait(send_sems, stage, piece)

    return begin, relay, arrived, settle


FIRST = 4.0 / 3.0
RATIO = 1.0 / 16.0
REACH = 2
GROUP = 4


def split(value):
    high = value.astype(jnp.bfloat16)
    return high, (value - high.astype(jnp.float32)).astype(jnp.bfloat16)


def product(left, right, dims):
    left_high, left_low = left
    right_high, right_low = right

    def one(first, second):
        return lax.dot_general(first, second, (dims, ((), ())), preferred_element_type=jnp.float32)

    return one(left_high, right_high) + (one(left_high, right_low) + one(left_low, right_high))


def filter_kernel(
    bands, spaces, cell_total, states, packed, result, out, high, low, staged,
    local, near, far, mine, final, gram, pending, inverse, grids, last, cells, near_ids, near_pot,
    tables, base_send, base_recv, in_send, in_recv, keep_sems, halo_send, halo_recv, out_send,
    out_recv, store_sems, gram_send, gram_recv,
):
    planes, held, plane_cells = states.shape
    half = held // 2
    chunks = half // TILE
    span = 4 * planes
    share = plane_cells // bands
    tiles = plane_cells // LANES
    band = lax.axis_index("band")
    space = lax.axis_index("space")
    side = lax.rem(space, 2)
    partner = space + 1 - 2 * side
    outward = space + 4 * side - 2
    across = space - 4 * side + 2
    has_outward = jnp.logical_and(outward >= 0, outward < spaces)
    has_across = jnp.logical_and(across >= 0, across < spaces)

    def to(target_band, target_space):
        return {"band": target_band, "space": target_space}

    own, theirs = 1 + side, 2 - side
    potential = packed.at[0:TILE]
    ids = packed.at[TILE : 2 * TILE, 0:LANES]
    table = packed[2 * TILE :, 0:LANES]

    barrier = pltpu.get_barrier_semaphore()
    for turn in range(bands):
        target = lax.rem(band + turn, bands)
        if turn:
            pl.semaphore_signal(
                barrier, inc=1, device_id=to(target, space), device_id_type=MESH
            )
        pl.semaphore_signal(barrier, inc=1, device_id=to(target, partner), device_id_type=MESH)
    lines = spaces // 2
    for offset in range(1, lines):
        pl.semaphore_signal(
            barrier,
            inc=1,
            device_id=to(band, 2 * lax.rem(space // 2 + offset, lines) + side),
            device_id_type=MESH,
        )
    pl.semaphore_wait(barrier, 2 * bands + lines - 2)

    def slab(place):
        return pl.ds(place * planes, planes)

    def rows_of(part, chunk):
        return pl.ds(pl.multiple_of(part * half + chunk * TILE, TILE), TILE)

    def remote(source, landing, send_sem, recv_sem, target):
        return pltpu.make_async_remote_copy(
            src_ref=source,
            dst_ref=landing,
            send_sem=send_sem,
            recv_sem=recv_sem,
            device_id=to(band, target),
            device_id_type=MESH,
        )

    own_landing, passed_landing = 3 * (1 - side), 3 * side
    base_sends = []
    for kind, (source, landing) in enumerate(((ids, near_ids), (potential, near_pot))):
        base_sends.append(
            (
                remote(source, landing.at[own], base_send.at[kind, 0], base_recv.at[kind, 0], partner),
                remote(source, landing.at[own_landing], base_send.at[kind, 1], base_recv.at[kind, 1], outward),
                remote(
                    landing.at[theirs], landing.at[passed_landing],
                    base_send.at[kind, 2], base_recv.at[kind, 2], across,
                ),
            )
        )
    enter, keep, halo_own, halo_passed = [], [], [], []
    for chunk in range(chunks):
        grid = grids.at[0, chunk]
        kept = states.at[:, rows_of(side, chunk)]
        enter.append(
            remote(
                states.at[:, rows_of(1 - side, chunk)], grid.at[slab(own)],
                in_send.at[chunk], in_recv.at[chunk], partner,
            )
        )
        keep.append(pltpu.make_async_copy(kept, grid.at[slab(own)], keep_sems.at[chunk]))
        halo_own.append(
            remote(
                kept, grid.at[slab(own_landing)],
                halo_send.at[0, chunk], halo_recv.at[0, chunk], outward,
            )
        )
        halo_passed.append(
            remote(
                grid.at[slab(theirs)], grid.at[slab(passed_landing)],
                halo_send.at[1, chunk], halo_recv.at[1, chunk], across,
            )
        )

    def begin(chunk):
        enter[chunk].start()

        @pl.when(has_outward)
        def _():
            halo_own[chunk].start()

    for kind in range(2):
        base_sends[kind][0].start()

    @pl.when(has_outward)
    def _():
        for kind in range(2):
            base_sends[kind][1].start()

    for chunk in range(min(2, chunks)):
        begin(chunk)
    for chunk in range(chunks):
        keep[chunk].start()
    near_ids[own] = ids[...]
    near_pot[own] = potential[...]
    missing_places = ((0, space < 2), (3, space >= spaces - 2))
    for place, missing in missing_places:

        @pl.when(missing)
        def _():
            near_ids[place] = jnp.zeros(near_ids.shape[1:], jnp.float32)
            near_pot[place] = jnp.zeros(near_pot.shape[1:], jnp.float32)
            for chunk in range(chunks):
                for plane in range(place * planes, (place + 1) * planes):
                    grids[0, chunk, plane] = jnp.zeros((TILE, plane_cells), jnp.float32)

    patches = table.shape[0]
    source = lax.broadcasted_iota(jnp.int32, (LANES, 3 * LANES), 0)
    lane_of = lax.broadcasted_iota(jnp.int32, (LANES, 3 * LANES), 1)
    wanted = lane_of // LANES * NZ + lane_of % NZ
    spread = jnp.where(source == wanted, 1.0, 0.0).astype(jnp.float32)
    tables[...] = matmul(table, spread, ((1,), (0,)))

    for kind in range(2):
        base_sends[kind][0].wait_recv()

    @pl.when(has_across)
    def _():
        for kind in range(2):
            base_sends[kind][2].start()
        for kind in range(2):
            base_sends[kind][1].wait_recv()

    @pl.when(has_outward)
    def _():
        for kind in range(2):
            base_sends[kind][2].wait_recv()

    row_source = lax.broadcasted_iota(jnp.int32, (LANES, plane_cells), 0)
    row_lane = lax.broadcasted_iota(jnp.int32, (LANES, plane_cells), 1)
    row_spread = jnp.where(row_source == row_lane // NZ, 1.0, 0.0).astype(jnp.float32)

    def make_cells(place, carry):
        patch = matmul(near_ids[place], row_spread, ((1,), (0,)))
        zero = jnp.zeros(patch.shape, jnp.float32)

        def look(step, metric):
            rows = tables[pl.ds(pl.multiple_of(TILE * step, TILE), TILE), :]
            for row in range(TILE):
                here = patch == (TILE * step + row).astype(jnp.float32)
                metric = tuple(
                    jnp.where(
                        here,
                        jnp.concatenate(
                            [rows[row : row + 1, kind * LANES : (kind + 1) * LANES]] * tiles, axis=1
                        ),
                        value,
                    )
                    for kind, value in enumerate(metric)
                )
            return metric

        metric = lax.fori_loop(0, patches // TILE, look, (zero, zero, zero))
        kinetic = [value * (-1.0 / HALF_WIDTH) for value in metric]
        centre = (near_pot[place] - CENTRE) * (2.0 / HALF_WIDTH) + WEIGHTS[2] * (
            kinetic[0] + kinetic[1] + kinetic[2]
        )
        for kind, value in enumerate([centre] + [FIRST * value for value in kinetic]):
            for plane in range(planes):
                cells[place * planes + plane, kind : kind + 1] = value[plane : plane + 1]
        return carry

    lax.fori_loop(0, 4, make_cells, 0)
    for place, missing in missing_places:

        @pl.when(missing)
        def _():
            for plane in range(place * planes, (place + 1) * planes):
                cells[plane] = jnp.zeros(cells.shape[1:], jnp.float32)

    start_factor(pending, pending.shape[0])
    lane = lax.broadcasted_iota(jnp.int32, (TILE, LANES), 1)
    depth_at = lane % NZ
    zero_tile = jnp.zeros((TILE, LANES), jnp.float32)

    def mask(inside, weight):
        return jnp.where(inside, weight, 0.0).astype(jnp.float32)

    back_one, fore_one = mask(depth_at >= 1, 1.0), mask(depth_at < NZ - 1, 1.0)
    back_two, fore_two = mask(depth_at >= 2, RATIO), mask(depth_at < NZ - 2, RATIO)
    first_row, front_half, not_last = lane < NZ, lane < 2 * NZ, lane < 3 * NZ

    def roll(value, amount):
        return pltpu.roll(value, amount, axis=1)

    def apply(step, chunk):
        edge = REACH * (step + 1)

        def some_planes(number, carry):
            first = edge + GROUP * number
            results = []
            state = []
            for k in range(GROUP):
                value = grids[step, chunk, first + k, :, 0:LANES]
                state.append((value, zero_tile, roll(value, 2 * NZ), roll(value, 3 * NZ), zero_tile))
            for tile in range(tiles):
                columns = slice(tile * LANES, (tile + 1) * LANES)
                for k in range(GROUP):
                    here = first + k
                    value, two_before, two_here, one_after, one_before = state[k]
                    one_here = roll(value, NZ)
                    if tile < tiles - 1:
                        following = grids[step, chunk, here, :, (tile + 1) * LANES : (tile + 2) * LANES]
                        two_after, one_next = roll(following, 2 * NZ), roll(following, 3 * NZ)
                    else:
                        following, two_after, one_next = None, zero_tile, zero_tile
                    state[k] = (following, two_here, two_after, one_next, one_here)

                    def plane(shift):
                        return grids[step, chunk, here + shift, :, columns]

                    def cell(kind):
                        return cells[here, kind : kind + 1, columns]

                    total = cell(0) * value
                    total = total + cell(1) * (
                        (plane(-1) + plane(1)) - (plane(-2) + plane(2)) * RATIO
                    )
                    near = jnp.where(first_row, one_before, one_here) + jnp.where(
                        not_last, one_after, one_next
                    )
                    far = two_here + jnp.where(front_half, two_before, two_after)
                    total = total + cell(2) * (near - far * RATIO)
                    along = (back_one * roll(value, 1) + fore_one * roll(value, LANES - 1)) - (
                        back_two * roll(value, 2) + fore_two * roll(value, LANES - 2)
                    )
                    total = total + cell(3) * along
                    if step > 0:
                        total = total - grids[step - 1, chunk, here, :, columns]
                    else:
                        total = total * 0.5
                    results.append((here, columns, total))
            for here, columns, total in results:
                if step < DEGREE - 1:
                    grids[step + 1, chunk, here, :, columns] = total
                else:
                    last[chunk, here - planes, :, columns] = total
            return carry

        lax.fori_loop(0, (span - 2 * edge) // GROUP, some_planes, 0)

    def leave(chunk):
        rows = pl.ds(pl.multiple_of(band * held + side * half + chunk * TILE, TILE), TILE)
        for turn in [*range(2, bands), *range(min(2, bands))]:
            target = lax.rem(band + turn, bands)
            columns = pl.ds(pl.multiple_of(target * share, share), share)
            for other in (1, 0):
                source = last.at[chunk, slab(side if other == 0 else 1 - side), :, columns]
                landing = out.at[:, rows, :]
                if turn == 0 and other == 0:
                    pltpu.make_async_copy(source, landing, out_recv.at[0]).start()
                else:
                    pltpu.make_async_remote_copy(
                        src_ref=source,
                        dst_ref=landing,
                        send_sem=out_send.at[0],
                        recv_sem=out_recv.at[0],
                        device_id=to(target, space if other == 0 else partner),
                        device_id_type=MESH,
                    ).start()

    def finish(chunk):
        @pl.when(has_across)
        def _():
            halo_own[chunk].wait_recv()

        @pl.when(has_outward)
        def _():
            halo_passed[chunk].wait_recv()

        for step in range(DEGREE):
            apply(step, chunk)
        leave(chunk)

    for chunk in range(chunks):
        keep[chunk].wait()
        enter[chunk].wait_recv()

        @pl.when(has_across)
        def _():
            halo_passed[chunk].start()

        if chunk + 2 < chunks:
            begin(chunk + 2)
        if chunk > 0:
            finish(chunk - 1)
    finish(chunks - 1)

    for kind in range(2):
        base_sends[kind][0].wait_send()
    for chunk in range(chunks):
        enter[chunk].wait_send()

    @pl.when(has_outward)
    def _():
        for kind in range(2):
            base_sends[kind][1].wait_send()
        for chunk in range(chunks):
            halo_own[chunk].wait_send()

    @pl.when(has_across)
    def _():
        for kind in range(2):
            base_sends[kind][2].wait_send()
        for chunk in range(chunks):
            halo_passed[chunk].wait_send()

    pltpu.make_async_copy(out, out, out_recv.at[0]).wait()
    size = out.shape[1]
    middle = size // 2
    for plane in range(planes):
        high[plane], low[plane] = split(out[plane])

    def gram_of(first, last):
        begin = first // LANES * LANES
        sums = None
        for plane in range(planes):
            term = product(
                (high[plane, first:last], low[plane, first:last]),
                (high[plane, begin:], low[plane, begin:]),
                ((1,), (1,)),
            )
            sums = term if sums is None else sums + term
        return sums

    begin, relay, arrived, settle = start_reduction(
        bands, spaces, cell_total, local, near, far, mine, final, gram, gram_send, gram_recv
    )
    pieces = near.shape[0]
    depth = near.shape[2] * 2 * bands
    folded = pieces * depth < size
    first_rows = gram_of(0, 2 * depth if folded else depth)
    local[:depth] = first_rows[:depth]
    begin(0)
    if folded:
        in_front = lax.broadcasted_iota(jnp.int32, (depth, LANES), 1) < depth
        second = first_rows[depth:]
        both = gram_of(2 * depth, 4 * depth)
        local[depth : 2 * depth, :LANES] = jnp.where(
            in_front, pltpu.roll(both[depth:], depth, axis=1), second[:, :LANES]
        )
        local[depth : 2 * depth, LANES:] = second[:, LANES:]
        local[2 * depth : 3 * depth, middle:] = both[:depth]
    else:
        for piece in range(1, pieces):
            local[piece * depth : (piece + 1) * depth, piece * depth // LANES * LANES :] = gram_of(
                piece * depth, (piece + 1) * depth
            )
    for piece in range(1, pieces):
        begin(piece)
    relay()
    stores = []
    for first in range(0, size, BLOCK):
        piece = first // depth
        if first % depth == 0 and piece < pieces:
            arrived(piece)
        if piece < pieces:
            rows = gram[first : first + BLOCK, first // LANES * LANES :]
        else:
            rows = pltpu.roll(gram[depth : 2 * depth, :LANES], depth, axis=1)
        if first == middle:
            top = split(inverse[:middle, :middle])
            for plane in range(planes):
                result[plane, :middle] = product(
                    top, (high[plane, :middle], low[plane, :middle]), ((1,), (0,))
                )
        factor_rows(rows, pending, inverse, first, size)
    bottom = split(inverse[middle:, :])
    for plane in range(planes):
        result[plane, middle:] = product(bottom, (high[plane], low[plane]), ((1,), (0,)))
    settle()
    for copy in stores:
        copy.wait()
    sent = out.at[:, 0 : out.shape[1] - out.shape[1] // (2 * bands), :]
    pltpu.make_async_copy(sent, sent, out_send.at[0]).wait()


def on_device(states, patch_ids, metric_table, potential):
    held, planes, plane_cells = states.shape
    bands = lax.axis_size("band")
    spaces = lax.axis_size("space")
    chunks = held // 2 // TILE
    total = held * bands
    depth = max(BLOCK, 2 * bands * TILE)
    folded = depth == BLOCK and total == 4 * BLOCK and LANES == 2 * BLOCK
    pieces = total // depth - int(folded)
    share = depth // (2 * bands)
    if planes != REACH * DEGREE:
        raise ValueError("slab depth")
    dma = pltpu.SemaphoreType.DMA
    hbm = pl.BlockSpec(memory_space=pltpu.HBM)
    regrouped = (planes, total, plane_cells // bands)
    height = 2 * TILE + metric_table.shape[0]
    packed = None
    for first, values in ((0, potential), (TILE, patch_ids), (2 * TILE, metric_table)):
        rows, columns = values.shape
        placed = jnp.pad(
            values, ((first, height - first - rows), (0, plane_cells - columns))
        ).astype(jnp.float32)
        packed = placed if packed is None else packed + placed
    result = pl.pallas_call(
        functools.partial(filter_kernel, bands, spaces, float(planes * plane_cells * spaces)),
        out_shape=jax.ShapeDtypeStruct(regrouped, jnp.float32),
        in_specs=[hbm, pl.BlockSpec(memory_space=pltpu.VMEM)],
        out_specs=pl.BlockSpec(memory_space=pltpu.VMEM),
        scratch_shapes=[
            pltpu.VMEM(regrouped, jnp.float32),
            pltpu.VMEM(regrouped, jnp.bfloat16),
            pltpu.VMEM(regrouped, jnp.bfloat16),
            pltpu.VMEM(regrouped, jnp.float32),
            pltpu.VMEM((total, total), jnp.float32),
            pltpu.VMEM((pieces, 2 * bands - 1, share, total), jnp.float32),
            pltpu.VMEM((pieces, spaces // 2, share, total), jnp.float32),
            pltpu.VMEM((pieces, share, total), jnp.float32),
            pltpu.VMEM((pieces, share, total), jnp.float32),
            pltpu.VMEM((total, total), jnp.float32),
            pltpu.VMEM((total, 2 * total), jnp.float32),
            pltpu.VMEM((total, total), jnp.float32),
            pltpu.VMEM((DEGREE, chunks, 4 * planes, TILE, plane_cells), jnp.float32),
            pltpu.VMEM((chunks, 2 * planes, TILE, plane_cells), jnp.float32),
            pltpu.VMEM((4 * planes, 4, plane_cells), jnp.float32),
            pltpu.VMEM((4, TILE, LANES), jnp.float32),
            pltpu.VMEM((4, TILE, plane_cells), jnp.float32),
            pltpu.VMEM((metric_table.shape[0], 3 * LANES), jnp.float32),
            dma((2, 3)),
            dma((2, 3)),
            dma((chunks,)),
            dma((chunks,)),
            dma((chunks,)),
            dma((2, chunks)),
            dma((2, chunks)),
            dma((1,)),
            dma((1,)),
            dma((2, planes)),
            dma((3, pieces)),
            dma((3, pieces)),
        ],
        compiler_params=pltpu.CompilerParams(
            collective_id=0, has_side_effects=True, vmem_limit_bytes=52 * 2**20
        ),
        name="orthonormal_states",
    )(states.transpose(1, 0, 2), packed)
    return result.transpose(1, 0, 2)


def solution(mesh):
    return jax.shard_map(
        on_device,
        mesh=mesh,
        in_specs=(P("band", "space", None), P("space", None), P(), P("space", None)),
        out_specs=P(None, "space", "band"),
        check_vma=False,
    )
```
